1024 devices in a mesh: dp: 8 (over y, x_hi), vocab: 32 (over z), mp: 4 (over x_lo, core).
Axes of the slice: x: 4 (x_hi: 2, x_lo: 2; x = x_hi * 2 + x_lo), y: 4, z: 32, core: 2. Of those that a mesh axis runs over, the one named last changes fastest.
Arguments:
- hidden: bfloat16 [1024, 3584], P('dp', 'mp'), may hold values from -20 to 20
- head_weight: bfloat16 [3584, 152064], P('mp', ('dp', 'vocab')), may hold values from -1 to 1
- teacher_logits: bfloat16 [1024, 152064], P('mp', ('dp', 'vocab')), may hold values from -20 to 330
- response_start: int32 [4], replicated, may hold values from 0 to 128
Outputs:
- token_kl: float32 [1024], P('mp')
- grad_hidden: float32 [1024, 3584], P('dp', 'mp')
- grad_head: bfloat16 [3584, 152064], P('mp', ('dp', 'vocab'))
The draws below stay inside these ranges and needn't reach their ends.
All inputs are finite; a program needn't handle non-finite values.
Results may differ from the reference program's by a relative error of at most 0.01.
Values may be sent and summed in bfloat16 or wider, within the bound.
A program may use at most 32 MiB of HBM per device.

```python
import jax
import jax.numpy as jnp

D = 3584
V = 152064
LEN = 256
TOKENS = 1024
SEQS = 4


def draw_hidden(key, part):
    noise_draw = jnp.clip(jax.random.normal(jax.random.fold_in(key, 11), (TOKENS, D), jnp.float32), -6.0, 6.0)
    return noise_draw.astype(jnp.bfloat16)


def draw_head_weight(key, part):
    weights = 0.05 * jnp.clip(jax.random.normal(jax.random.fold_in(key, 17), (D, V), jnp.float32), -6.0, 6.0)
    return weights.astype(jnp.bfloat16)


def draw_teacher_logits(key, part):
    base_draw = 3.0 * jnp.clip(jax.random.normal(jax.random.fold_in(key, 19), (TOKENS, V), jnp.float32), -6.0, 6.0)
    return base_draw.astype(jnp.bfloat16)


def with_ends(array, key, least, top_value):
    dims = array.shape
    index_at = [jax.random.randint(jax.random.fold_in(key, axis), (), 0, dims[axis]) for axis in range(len(dims))]
    array = array.at[tuple(index_at)].set(least)
    longest = dims.index(max(dims))
    index_at[longest] = (index_at[longest] + 1) % dims[longest]
    return array.at[tuple(index_at)].set(top_value)


def setup_inputs(seed: int = 0) -> dict:
    keys = jax.random.split(jax.random.key(seed), 5)
    return {
        "hidden": draw_hidden(jax.random.fold_in(keys[4], 71), 0),
        "head_weight": draw_head_weight(jax.random.fold_in(keys[4], 71), 0),
        "teacher_logits": draw_teacher_logits(jax.random.fold_in(keys[4], 71), 0),
        "response_start": with_ends(jax.random.randint(keys[3], (SEQS,), 0, LEN // 2 + 1), jax.random.fold_in(keys[3], 1), 0, (LEN // 2 + 1) - 1).astype(jnp.int32),
    }


def reference(hidden, head_weight, teacher_logits, response_start):
    student = jnp.dot(hidden, head_weight, preferred_element_type=jnp.float32)
    target = teacher_logits.astype(jnp.float32)
    top_s = jnp.max(student, axis=1, keepdims=True)
    top_t = jnp.max(target, axis=1, keepdims=True)
    exp_s = jnp.exp(student - top_s)
    exp_t = jnp.exp(target - top_t)
    sum_s = jnp.sum(exp_s, axis=1)
    sum_t = jnp.sum(exp_t, axis=1)
    cross_term = jnp.sum(exp_t * (target - student), axis=1)
    positions = jnp.arange(TOKENS, dtype=jnp.int32)
    sequence = positions // LEN
    starts = response_start[sequence]
    response_mask = (positions % LEN >= starts).astype(jnp.float32)
    token_kl = response_mask * (cross_term / sum_t - top_t[:, 0] - jnp.log(sum_t) + top_s[:, 0] + jnp.log(sum_s))
    logit_grads = (response_mask[:, None] * (exp_s / sum_s[:, None] - exp_t / sum_t[:, None])).astype(jnp.bfloat16)
    grad_head = jnp.dot(hidden.T, logit_grads, preferred_element_type=jnp.float32).astype(jnp.bfloat16)
    grad_hidden = jnp.dot(logit_grads, head_weight.T, preferred_element_type=jnp.float32)
    return token_kl, grad_hidden, grad_head
```

```python
import functools

import jax
import jax.numpy as jnp
from jax import lax
from jax.experimental import pallas as pl
from jax.experimental.pallas import tpu as pltpu
from jax.sharding import PartitionSpec as P

LEN = 256
MESH = pl.DeviceIdType.MESH
F32 = jnp.float32
BF16 = jnp.bfloat16

ROW_MS, ROW_SS, ROW_MT, ROW_ST, ROW_C = range(5)


class Group:
    def __init__(self, n, me, device):
        self.n, self.me, self.device = n, me, device

    def others(self):
        return [lax.rem(self.me + k, self.n) for k in range(1, self.n)]

    def copy(self, src, dst, send, recv, to):
        return pltpu.make_async_remote_copy(
            src_ref=src,
            dst_ref=dst,
            send_sem=send,
            recv_sem=recv,
            device_id=self.device(to),
            device_id_type=MESH,
        )


def gather_start(group, src, held, send, recv):
    for peer in group.others():
        group.copy(src, held.at[group.me], send.at[peer], recv.at[group.me], peer).start()


def gather_wait(group, src, held, send, recv):
    for peer in group.others():
        copy = group.copy(src, held.at[peer], send.at[peer], recv.at[peer], peer)
        copy.wait_recv()
        copy.wait_send()


def scatter_start(group, parts, held, send, recv):
    for peer in group.others():
        group.copy(parts.at[peer], held.at[group.me], send.at[peer], recv.at[group.me], peer).start()


def scatter_wait(group, parts, held, send, recv):
    for peer in group.others():
        copy = group.copy(parts.at[peer], held.at[peer], send.at[peer], recv.at[peer], peer)
        copy.wait_recv()
        copy.wait_send()


def merge(held, n):
    rows = [[held[i, r : r + 1, :] for r in range(5)] for i in range(n)]
    top_s = functools.reduce(jnp.maximum, [row[ROW_MS] for row in rows])
    top_t = functools.reduce(jnp.maximum, [row[ROW_MT] for row in rows])
    sum_s = sum_t = cross = None
    for row in rows:
        scale_s = jnp.exp(row[ROW_MS] - top_s)
        scale_t = jnp.exp(row[ROW_MT] - top_t)
        terms = row[ROW_SS] * scale_s, row[ROW_ST] * scale_t, row[ROW_C] * scale_t
        if sum_s is None:
            sum_s, sum_t, cross = terms
        else:
            sum_s, sum_t, cross = sum_s + terms[0], sum_t + terms[1], cross + terms[2]
    return top_s, sum_s, top_t, sum_t, cross


def store_stats(ref, stats):
    for row, value in enumerate(stats):
        ref[row : row + 1, :] = value


def kernel(
    sizes,
    hidden_ref, head_ref, teacher_ref, start_ref,
    kl_ref, grad_hidden_ref, grad_head_ref,
    hid, keep, swap_out, swap_in, cross_out, cross_in, stud,
    st_dp, st_zl, st_zh, grads, gh_out, gh_in, acc,
    zl_out, zl_in, zh_out, zh_in, fin_h, fin_l, head_acc,
    local_sem, hid_s, hid_r, swap_s, swap_r, cross_s, cross_r,
    sdp_s, sdp_r, szl_s, szl_r, szh_s, szh_r,
    gx_s, gx_r, gc_s, gc_r, gd_s, gd_r, gh_s, gh_r,
    zl_s, zl_r, zh_s, zh_r, fh_s, fh_r, fl_s, fl_r,
):
    n_dp, n_zl, n_zh = sizes
    tok = hidden_ref.shape[0]
    d, z, m = lax.axis_index("dp"), lax.axis_index("vocab"), lax.axis_index("mp")
    x, c = m // 2, m % 2
    zl, zh = z % n_zl, z // n_zl
    other_core, other_chip = 2 * x + (1 - c), 2 * (1 - x) + c
    diagonal = 2 * (1 - x) + (1 - c)

    dp = Group(n_dp, d, lambda i: (i, z, m))
    near = Group(n_zl, zl, lambda i: (d, zh * n_zl + i, m))
    far = Group(n_zh, zh, lambda i: (d, i * n_zl + zl, m))
    mp = Group(4, m, lambda i: (d, z, i))

    barrier = pltpu.get_barrier_semaphore()
    peers = [g.device(p) for g in (dp, near, far) for p in g.others()]
    peers += [mp.device(other_core), mp.device(other_chip)]
    for peer in peers:
        pl.semaphore_signal(barrier, inc=1, device_id=peer, device_id_type=MESH)
    own = pltpu.make_async_copy(hidden_ref, hid.at[d], local_sem)
    own.start()
    pl.semaphore_wait(barrier, len(peers))

    gather_start(dp, hidden_ref, hid, hid_s, hid_r)

    own.wait()
    gather_wait(dp, hidden_ref, hid, hid_s, hid_r)

    def swap(k):
        return mp.copy(swap_out.at[k], swap_in.at[k], swap_s.at[k], swap_r.at[k], other_core)

    def cross(k):
        return mp.copy(cross_out.at[k], cross_in.at[k], cross_s.at[k], cross_r.at[k], other_chip)

    def partial(block):
        return lax.dot_general(
            head_ref[...], hid[block], (((1,), (1,)), ((), ())), preferred_element_type=F32
        )

    def student_step(k, carry):
        half = k % 2
        chip = jnp.where(k < 2, 1 - x, x)
        swap_out[k] = partial(2 * (2 * chip + 1 - c) + half)
        swap(k).start()
        keep[k] = partial(2 * (2 * chip + c) + half)
        return carry

    lax.fori_loop(0, 4, student_step, 0)
    for k in range(2):
        swap(k).wait()
        cross_out[k] = keep[k] + swap_in[k]
        cross(k).start()
    for k in range(2):
        swap(2 + k).wait()
        keep[2 + k] = keep[2 + k] + swap_in[2 + k]

    for h in range(2):
        cols = slice(h * tok, (h + 1) * tok)
        cross(h).wait()
        s = keep[2 + h] + cross_in[h]
        stud[h] = s
        t = teacher_ref[:, cols].astype(F32)
        top_s = jnp.max(s, axis=0, keepdims=True)
        top_t = jnp.max(t, axis=0, keepdims=True)
        exp_t = jnp.exp(t - top_t)
        stats = (
            top_s,
            jnp.sum(jnp.exp(s - top_s), axis=0, keepdims=True),
            top_t,
            jnp.sum(exp_t, axis=0, keepdims=True),
            jnp.sum(exp_t * (t - s), axis=0, keepdims=True),
        )
        for row, value in enumerate(stats):
            st_dp[d, row : row + 1, cols] = value
    for group, held, send, recv, to in (
        (dp, st_dp, sdp_s, sdp_r, st_zl.at[zl]),
        (near, st_zl, szl_s, szl_r, st_zh.at[zh]),
        (far, st_zh, szh_s, szh_r, None),
    ):
        gather_start(group, held.at[group.me], held, send, recv)
        gather_wait(group, held.at[group.me], held, send, recv)
        stats = merge(held, group.n)
        if to is not None:
            store_stats(to, stats)
    top_s, sum_s, top_t, sum_t, cross_term = stats
    position = lax.broadcasted_iota(jnp.int32, (1, 2 * tok), 1)
    mask = jnp.where(position >= start_ref[m], 1.0, 0.0).astype(F32)
    kl_ref[...] = mask * (cross_term / sum_t - top_t - jnp.log(sum_t) + top_s + jnp.log(sum_s))
    scale_s, scale_t = mask / sum_s, mask / sum_t

    def grad_x(h):
        block = grads.at[2 * m + h]
        return mp.copy(block, block, gx_s.at[h], gx_r.at[h], other_chip)

    def grad_c(h):
        block = grads.at[2 * m + h]
        return mp.copy(block, block, gc_s.at[h], gc_r.at[h], other_core)

    def grad_d(h):
        block = grads.at[2 * other_chip + h]
        return mp.copy(block, block, gd_s.at[h], gd_r.at[h], other_core)

    for h in range(2):
        cols = slice(h * tok, (h + 1) * tok)
        exp_s = jnp.exp(stud[h] - top_s[:, cols])
        exp_t = jnp.exp(teacher_ref[:, cols].astype(F32) - top_t[:, cols])
        grads[2 * m + h] = (exp_s * scale_s[:, cols] - exp_t * scale_t[:, cols]).astype(BF16)
        grad_x(h).start()
        grad_c(h).start()

    def owner_copy(block):
        return dp.copy(gh_out.at[block], gh_in.at[d], gh_s.at[block], gh_r.at[d], block)

    def hidden_terms(block):
        gh_out[block] = lax.dot_general(
            grads[block], head_ref[...], (((0,), (0,)), ((), ())), preferred_element_type=F32
        ).astype(BF16)

        @pl.when(block != d)
        def _():
            owner_copy(block).start()

    for h in range(2):
        hidden_terms(2 * m + h)
    for h in range(2):
        grad_c(h).wait()
        hidden_terms(2 * other_core + h)
    for h in range(2):
        grad_x(h).wait()
        grad_d(h).start()
        hidden_terms(2 * other_chip + h)
    for h in range(2):
        grad_d(h).wait()
        hidden_terms(2 * diagonal + h)

    head_acc[...] = jnp.zeros_like(head_acc)

    def head_step(block, carry):
        head_acc[...] += jnp.dot(grads[block], hid[block], preferred_element_type=F32)
        return carry

    lax.fori_loop(0, n_dp, head_step, 0)
    grad_head_ref[...] = head_acc[...].astype(BF16)

    scatter_wait(dp, gh_out, gh_in, gh_s, gh_r)
    gh_in[d] = gh_out[d]
    total = gh_in[0].astype(F32)
    for i in range(1, n_dp):
        total = total + gh_in[i].astype(F32)

    rows = tok // n_zl
    for i in range(n_zl):
        acc[i] = total[i * rows : (i + 1) * rows, :]
        zl_out[i] = acc[i].astype(BF16)
    scatter_start(near, zl_out, zl_in, zl_s, zl_r)
    scatter_wait(near, zl_out, zl_in, zl_s, zl_r)
    total = acc[zl]
    for peer in near.others():
        total = total + zl_in[peer].astype(F32)
    few = rows // n_zh
    for i in range(n_zh):
        zh_out[i] = total[i * few : (i + 1) * few, :]
    scatter_start(far, zh_out, zh_in, zh_s, zh_r)
    scatter_wait(far, zh_out, zh_in, zh_s, zh_r)
    zh_in[zh] = zh_out[zh]
    total = zh_in[0]
    for i in range(1, n_zh):
        total = total + zh_in[i]
    fin_h[zh] = total
    gather_start(far, fin_h.at[zh], fin_h, fh_s, fh_r)
    gather_wait(far, fin_h.at[zh], fin_h, fh_s, fh_r)
    for i in range(n_zh):
        fin_l[zl, i * few : (i + 1) * few, :] = fin_h[i]
    gather_start(near, fin_l.at[zl], fin_l, fl_s, fl_r)
    gather_wait(near, fin_l.at[zl], fin_l, fl_s, fl_r)
    for i in range(n_zl):
        grad_hidden_ref[i * rows : (i + 1) * rows, :] = fin_l[i]


def solution(mesh):
    n_dp, n_z, n_mp = mesh.shape["dp"], mesh.shape["vocab"], mesh.shape["mp"]
    n_zl = min(4, n_z)
    n_zh = n_z // n_zl

    def per_device(hidden, head_weight, teacher_logits, response_start):
        tok, depth = hidden.shape
        own, cols = teacher_logits.shape
        assert n_mp == 4 and own == 2 * tok == LEN and n_dp == 8
        rows = tok // n_zl
        few = rows // n_zh
        dma = pltpu.SemaphoreType.DMA
        vmem = pl.BlockSpec(memory_space=pltpu.VMEM)
        kl, grad_hidden, grad_head = pl.pallas_call(
            functools.partial(kernel, (n_dp, n_zl, n_zh)),
            name="distill",
            out_shape=(
                jax.ShapeDtypeStruct((1, own), F32),
                jax.ShapeDtypeStruct((tok, depth), F32),
                jax.ShapeDtypeStruct((cols, depth), BF16),
            ),
            in_specs=[vmem, vmem, vmem, pl.BlockSpec(memory_space=pltpu.SMEM)],
            out_specs=(vmem, vmem, vmem),
            scratch_shapes=[
                pltpu.VMEM((n_dp, tok, depth), BF16),
                pltpu.VMEM((4, cols, tok), F32),
                pltpu.VMEM((4, cols, tok), F32),
                pltpu.VMEM((4, cols, tok), F32),
                pltpu.VMEM((2, cols, tok), F32),
                pltpu.VMEM((2, cols, tok), F32),
                pltpu.VMEM((2, cols, tok), F32),
                pltpu.VMEM((n_dp, 8, own), F32),
                pltpu.VMEM((n_zl, 8, own), F32),
                pltpu.VMEM((n_zh, 8, own), F32),
                pltpu.VMEM((n_dp, cols, tok), BF16),
                pltpu.VMEM((n_dp, tok, depth), BF16),
                pltpu.VMEM((n_dp, tok, depth), BF16),
                pltpu.VMEM((n_zl, rows, depth), F32),
                pltpu.VMEM((n_zl, rows, depth), BF16),
                pltpu.VMEM((n_zl, rows, depth), BF16),
                pltpu.VMEM((n_zh, few, depth), F32),
                pltpu.VMEM((n_zh, few, depth), F32),
                pltpu.VMEM((n_zh, few, depth), F32),
                pltpu.VMEM((n_zl, rows, depth), F32),
                pltpu.VMEM((cols, depth), F32),
                dma,
                dma((n_dp,)), dma((n_dp,)),
                dma((4,)), dma((4,)),
                dma((2,)), dma((2,)),
                dma((n_dp,)), dma((n_dp,)),
                dma((n_zl,)), dma((n_zl,)),
                dma((n_zh,)), dma((n_zh,)),
                dma((2,)), dma((2,)),
                dma((2,)), dma((2,)),
                dma((2,)), dma((2,)),
                dma((n_dp,)), dma((n_dp,)),
                dma((n_zl,)), dma((n_zl,)),
                dma((n_zh,)), dma((n_zh,)),
                dma((n_zh,)), dma((n_zh,)),
                dma((n_zl,)), dma((n_zl,)),
            ],
            compiler_params=pltpu.CompilerParams(
                collective_id=0, has_side_effects=True, vmem_limit_bytes=56 << 20
            ),
        )(hidden, head_weight.T, teacher_logits.T, response_start)
        return kl.reshape(own), grad_hidden, grad_head.T

    return jax.shard_map(
        per_device,
        mesh=mesh,
        in_specs=(P("dp", "mp"), P("mp", ("dp", "vocab")), P("mp", ("dp", "vocab")), P()),
        out_specs=(P("mp"), P("dp", "mp"), P("mp", ("dp", "vocab"))),
        check_vma=False,
    )
```

```python
import functools

import jax
import jax.numpy as jnp
from jax import lax
from jax.experimental import pallas as pl
from jax.experimental.pallas import tpu as pltpu
from jax.sharding import PartitionSpec as P

LEN = 256
MESH = pl.DeviceIdType.MESH
F32 = jnp.float32
BF16 = jnp.bfloat16

ROW_MS, ROW_SS, ROW_MT, ROW_ST, ROW_C = range(5)


class Group:
    def __init__(self, n, me, device):
        self.n, self.me, self.device = n, me, device

    def others(self):
        return [lax.rem(self.me + k, self.n) for k in range(1, self.n)]

    def copy(self, src, dst, send, recv, to):
        return pltpu.make_async_remote_copy(
            src_ref=src,
            dst_ref=dst,
            send_sem=send,
            recv_sem=recv,
            device_id=self.device(to),
            device_id_type=MESH,
        )


def gather_start(group, src, held, send, recv):
    for peer in group.others():
        group.copy(src, held.at[group.me], send.at[peer], recv.at[group.me], peer).start()


def gather_wait(group, src, held, send, recv):
    for peer in group.others():
        copy = group.copy(src, held.at[peer], send.at[peer], recv.at[peer], peer)
        copy.wait_recv()
        copy.wait_send()


def scatter_start(group, parts, held, send, recv):
    for peer in group.others():
        group.copy(parts.at[peer], held.at[group.me], send.at[peer], recv.at[group.me], peer).start()


def scatter_wait(group, parts, held, send, recv):
    for peer in group.others():
        copy = group.copy(parts.at[peer], held.at[peer], send.at[peer], recv.at[peer], peer)
        copy.wait_recv()
        copy.wait_send()


def merge(held, n):
    rows = [[held[i, r : r + 1, :] for r in range(5)] for i in range(n)]
    top_s = functools.reduce(jnp.maximum, [row[ROW_MS] for row in rows])
    top_t = functools.reduce(jnp.maximum, [row[ROW_MT] for row in rows])
    sum_s = sum_t = cross = None
    for row in rows:
        scale_s = jnp.exp(row[ROW_MS] - top_s)
        scale_t = jnp.exp(row[ROW_MT] - top_t)
        terms = row[ROW_SS] * scale_s, row[ROW_ST] * scale_t, row[ROW_C] * scale_t
        if sum_s is None:
            sum_s, sum_t, cross = terms
        else:
            sum_s, sum_t, cross = sum_s + terms[0], sum_t + terms[1], cross + terms[2]
    return top_s, sum_s, top_t, sum_t, cross


def store_stats(ref, stats):
    for row, value in enumerate(stats):
        ref[row : row + 1, :] = value


def kernel(
    sizes,
    hidden_ref, head_hbm, teacher_hbm, start_ref,
    kl_ref, grad_hidden_ref, grad_head_hbm,
    head_ref, teacher_ref, head_out,
    hid, parts, swap_in, cross_out, cross_in, stud,
    st_dp, st_zl, st_zh, grads, gh_out, gh_in, acc,
    zl_out, zl_in, zh_out, zh_in, fin_h, fin_f, fin_l, head_acc,
    local_sem, ready, hx_s, hx_r, hy_s, hy_r, hz_s, hz_r,
    swap_s, swap_r, cross_s, cross_r,
    sdp_s, sdp_r, szl_s, szl_r, szh_s, szh_r,
    gx_s, gx_r, gc_s, gc_r, gd_s, gd_r, gh_s, gh_r,
    zl_s, zl_r, zh_s, zh_r, fh_s, fh_r, fl_s, fl_r,
):
    n_dp, n_z, n_zl, n_zh = sizes
    n_y = n_dp // 2
    sub, depth = hidden_ref.shape[1:]
    tok = 4 * sub
    d, z, m = lax.axis_index("dp"), lax.axis_index("vocab"), lax.axis_index("mp")
    x, c = m // 2, m % 2
    y = d // 2
    partner = 2 * y + (1 - d % 2)
    zl, zh = z % n_zl, z // n_zl
    other_core, other_chip = 2 * x + (1 - c), 2 * (1 - x) + c
    diagonal = 2 * (1 - x) + (1 - c)
    up, down = lax.rem(z + 1, n_z), lax.rem(z + n_z - 1, n_z)

    dp = Group(n_dp, d, lambda i: (i, z, m))
    column = Group(n_y, y, lambda i: (2 * i + d % 2, z, m))
    ring = Group(n_z, z, lambda i: (d, i, m))
    near = Group(n_zl, zl, lambda i: (d, zh * n_zl + i, m))
    far = Group(n_zh, zh, lambda i: (d, i * n_zl + zl, m))
    mp = Group(4, m, lambda i: (d, z, i))
    far_next = [far.device(lax.rem(zh + k, n_zh)) for k in (1, n_zh - 1)]

    barrier = pltpu.get_barrier_semaphore()
    peers = [g.device(p) for g in (dp, near) for p in g.others()] + far_next
    peers += [mp.device(other_core), mp.device(other_chip), ring.device(up), ring.device(down)]
    for peer in peers:
        pl.semaphore_signal(barrier, inc=1, device_id=peer, device_id_type=MESH)
    own = pltpu.make_async_copy(hidden_ref, hid.at[d], local_sem.at[0])
    own.start()
    load_head = pltpu.make_async_copy(head_hbm, head_ref, local_sem.at[1])
    load_head.start()
    load_teacher = pltpu.make_async_copy(teacher_hbm, teacher_ref, local_sem.at[2])
    load_teacher.start()
    own.wait()
    pl.semaphore_wait(barrier, len(peers))

    def tell(r):
        for peer in far_next:
            pl.semaphore_signal(ready.at[r], inc=1, device_id=peer, device_id_type=MESH)

    def hear(r):
        pl.semaphore_wait(ready.at[r], 2)

    half = pl.ds(2 * (z % 2), 2)

    def to_partner(block):
        part = hid.at[block, half]
        return dp.copy(part, part, hx_s, hx_r, partner)

    def to_column(block, peer):
        part = hid.at[block, half]
        return column.copy(part, part, hy_s.at[block % 2, peer], hy_r.at[block], peer)

    def to_ring(block, side, parity):
        part = hid.at[block, 2 * parity + side]
        return ring.copy(part, part, hz_s.at[block, side], hz_r.at[block, side], (up, down)[side])

    def pass_on(block):
        for side in range(2):
            to_ring(block, side, z % 2).start()

    to_partner(d).start()
    for i in range(2):
        block = 2 * y + i

        @pl.when(block != d)
        def _():
            to_partner(partner).wait_recv()

        for peer in column.others():
            to_column(block, peer).start()
    pass_on(partner)
    if n_zh >= 4:
        tell(0)

    def blocks_of(i):
        return [2 * row + i for row in column.others()]

    def forward(i):
        for block in blocks_of(i):
            to_column(block, block // 2).wait_recv()
            pass_on(block)

    def arrive(i):
        for block in blocks_of(i):
            for side in range(2):
                to_ring(block, side, 1 - z % 2).wait_recv()

        @pl.when(2 * y + i != d)
        def _():
            for side in range(2):
                to_ring(partner, side, 1 - z % 2).wait_recv()

    def swap(k):
        return mp.copy(parts.at[k, 0], swap_in.at[k], swap_s.at[k], swap_r.at[k], other_core)

    def cross(k):
        return mp.copy(cross_out.at[k], cross_in.at[k], cross_s.at[k], cross_r.at[k], other_chip)

    def partial_sums(k):
        chip = (1 - x) if k < 2 else x

        def one(j, carry):
            core = jnp.where(j == 0, 1 - c, c)
            block = hid[2 * (2 * chip + core) + k % 2].reshape(tok, depth)
            parts[k, j] = lax.dot_general(
                head_ref[...], block, (((1,), (1,)), ((), ())), preferred_element_type=F32
            )
            return carry

        lax.fori_loop(0, 2, one, 0)
        swap(k).start()

    def send_cross(k):
        swap(k).wait()
        cross_out[k] = parts[k, 1] + swap_in[k]
        cross(k).start()

    forward(0)
    load_head.wait()
    arrive(0)
    partial_sums(0)
    send_cross(0)
    if n_zh >= 4:
        hear(0)
        tell(1)
    forward(1)
    arrive(1)
    partial_sums(1)
    send_cross(1)
    if n_zh >= 4:
        hear(1)
        tell(2)
    partial_sums(2)
    partial_sums(3)
    load_teacher.wait()

    for h in range(2):
        cols = slice(h * tok, (h + 1) * tok)
        swap(2 + h).wait()
        stud[h] = parts[2 + h, 1] + swap_in[2 + h]
        cross(h).wait()
        s = stud[h] + cross_in[h]
        stud[h] = s
        t = teacher_ref[:, cols].astype(F32)
        top_s = jnp.max(s, axis=0, keepdims=True)
        top_t = jnp.max(t, axis=0, keepdims=True)
        exp_t = jnp.exp(t - top_t)
        stats = (
            top_s,
            jnp.sum(jnp.exp(s - top_s), axis=0, keepdims=True),
            top_t,
            jnp.sum(exp_t, axis=0, keepdims=True),
            jnp.sum(exp_t * (t - s), axis=0, keepdims=True),
        )
        for row, value in enumerate(stats):
            st_dp[d, row : row + 1, cols] = value

    def share(group, held, send, recv):
        gather_start(group, held.at[group.me], held, send, recv)
        gather_wait(group, held.at[group.me], held, send, recv)
        return merge(held, group.n)

    store_stats(st_zl.at[zl], share(dp, st_dp, sdp_s, sdp_r))
    store_stats(st_zh.at[zh], share(near, st_zl, szl_s, szl_r))
    if n_zh >= 4:
        hear(2)
    top_s, sum_s, top_t, sum_t, cross_term = share(far, st_zh, szh_s, szh_r)
    position = lax.broadcasted_iota(jnp.int32, (1, 2 * tok), 1)
    mask = jnp.where(position >= start_ref[m], 1.0, 0.0).astype(F32)
    scale_s, scale_t = mask / sum_s, mask / sum_t

    def grad_x():
        return mp.copy(grads.at[m], grads.at[m], gx_s, gx_r, other_chip)

    def grad_c():
        return mp.copy(grads.at[m], grads.at[m], gc_s, gc_r, other_core)

    def grad_d():
        return mp.copy(grads.at[other_chip], grads.at[other_chip], gd_s, gd_r, other_core)

    for h in range(2):
        cols = slice(h * tok, (h + 1) * tok)
        exp_s = jnp.exp(stud[h] - top_s[:, cols])
        exp_t = jnp.exp(teacher_ref[:, cols].astype(F32) - top_t[:, cols])
        grads[m, :, cols] = (exp_s * scale_s[:, cols] - exp_t * scale_t[:, cols]).astype(BF16)
    grad_x().start()
    grad_c().start()
    kl_ref[...] = mask * (cross_term / sum_t - top_t - jnp.log(sum_t) + top_s + jnp.log(sum_s))

    def owner_copy(block):
        return dp.copy(gh_out.at[block], gh_in.at[d], gh_s.at[block], gh_r.at[d], block)

    def hidden_terms(quarter):
        for h in range(2):
            block = 2 * quarter + h
            gh_out[block] = lax.dot_general(
                grads[quarter, :, h * tok : (h + 1) * tok],
                head_ref[...],
                (((0,), (0,)), ((), ())),
                preferred_element_type=F32,
            ).astype(BF16)

            @pl.when(block != d)
            def _():
                owner_copy(block).start()

    hidden_terms(m)
    grad_c().wait()
    hidden_terms(other_core)
    grad_x().wait()
    grad_d().start()
    hidden_terms(other_chip)
    grad_d().wait()
    hidden_terms(diagonal)

    scatter_wait(dp, gh_out, gh_in, gh_s, gh_r)
    gh_in[d] = gh_out[d]
    total = gh_in[0].astype(F32)
    for i in range(1, n_dp):
        total = total + gh_in[i].astype(F32)

    rows = tok // n_zl
    for i in range(n_zl):
        acc[i] = total[i * rows : (i + 1) * rows, :]
        zl_out[i] = acc[i].astype(BF16)
    scatter_start(near, zl_out, zl_in, zl_s, zl_r)
    scatter_wait(near, zl_out, zl_in, zl_s, zl_r)
    total = acc[zl]
    for peer in near.others():
        total = total + zl_in[peer].astype(F32)
    few = rows // n_zh
    for i in range(n_zh):
        zh_out[i] = total[i * few : (i + 1) * few, :].astype(BF16)
    scatter_start(far, zh_out, zh_in, zh_s, zh_r)

    def head_step(quarter, carry):
        tokens = hid[pl.ds(2 * quarter, 2)].reshape(2 * tok, depth)
        head_acc[...] += jnp.dot(grads[quarter], tokens, preferred_element_type=F32)
        return carry

    head_acc[...] = jnp.zeros_like(head_acc)
    lax.fori_loop(0, n_y, head_step, 0)
    head_out[...] = head_acc[...].astype(BF16)
    store_head = pltpu.make_async_copy(head_out, grad_head_hbm, local_sem.at[3])
    store_head.start()

    scatter_wait(far, zh_out, zh_in, zh_s, zh_r)
    zh_in[zh] = zh_out[zh]
    total = zh_in[0].astype(F32)
    for i in range(1, n_zh):
        total = total + zh_in[i].astype(F32)
    fin_h[zh] = total.astype(BF16)
    gather_start(far, fin_h.at[zh], fin_h, fh_s, fh_r)
    gather_wait(far, fin_h.at[zh], fin_h, fh_s, fh_r)
    for i in range(n_zh):
        fin_f[i * few : (i + 1) * few, :] = fin_h[i].astype(F32)
    fin_l[zl] = fin_f[...].astype(BF16)
    gather_start(near, fin_l.at[zl], fin_l, fl_s, fl_r)
    gather_wait(near, fin_l.at[zl], fin_l, fl_s, fl_r)
    for i in range(n_zl):
        grad_hidden_ref[i * rows : (i + 1) * rows, :] = fin_l[i].astype(F32)

    to_partner(d).wait_send()
    for i in range(2):
        for peer in column.others():
            to_column(2 * y + i, peer).wait_send()
    for block in [partner] + blocks_of(0) + blocks_of(1):
        for side in range(2):
            to_ring(block, side, z % 2).wait_send()
    store_head.wait()


def copy_kernel(a, b, c, a_out, b_out, c_out, sems):
    copies = [
        pltpu.make_async_copy(src, dst, sems.at[i])
        for i, (src, dst) in enumerate(((a, a_out), (b, b_out), (c, c_out)))
    ]
    for copy in copies:
        copy.start()
    for copy in copies:
        copy.wait()


def solution(mesh):
    n_dp, n_z, n_mp = mesh.shape["dp"], mesh.shape["vocab"], mesh.shape["mp"]
    n_zl = min(4, n_z)
    n_zh = n_z // n_zl

    def per_device(hidden, head_weight, teacher_logits, response_start):
        tok, depth = hidden.shape
        own, cols = teacher_logits.shape
        assert n_mp == 4 and own == 2 * tok == LEN and n_dp == 8 and n_zh == 8
        rows = tok // n_zl
        few = rows // n_zh
        dma = pltpu.SemaphoreType.DMA
        vmem = pl.BlockSpec(memory_space=pltpu.VMEM)
        hbm = pl.BlockSpec(memory_space=pl.ANY)
        shapes = (
            jax.ShapeDtypeStruct((1, own), F32),
            jax.ShapeDtypeStruct((tok, depth), F32),
            jax.ShapeDtypeStruct((cols, depth), BF16),
        )
        results = pl.pallas_call(
            functools.partial(kernel, (n_dp, n_z, n_zl, n_zh)),
            name="distill",
            out_shape=shapes,
            in_specs=[hbm, hbm, hbm, pl.BlockSpec(memory_space=pltpu.SMEM)],
            out_specs=(vmem, vmem, hbm),
            scratch_shapes=[
                pltpu.VMEM((cols, depth), BF16),
                pltpu.VMEM((cols, own), BF16),
                pltpu.VMEM((cols, depth), BF16),
                pltpu.VMEM((n_dp, 4, tok // 4, depth), BF16),
                pltpu.VMEM((4, 2, cols, tok), F32),
                pltpu.VMEM((4, cols, tok), F32),
                pltpu.VMEM((2, cols, tok), F32),
                pltpu.VMEM((2, cols, tok), F32),
                pltpu.VMEM((2, cols, tok), F32),
                pltpu.VMEM((n_dp, 8, own), F32),
                pltpu.VMEM((n_zl, 8, own), F32),
                pltpu.VMEM((n_zh, 8, own), F32),
                pltpu.VMEM((4, cols, own), BF16),
                pltpu.VMEM((n_dp, tok, depth), BF16),
                pltpu.VMEM((n_dp, tok, depth), BF16),
                pltpu.VMEM((n_zl, rows, depth), F32),
                pltpu.VMEM((n_zl, rows, depth), BF16),
                pltpu.VMEM((n_zl, rows, depth), BF16),
                pltpu.VMEM((n_zh, few, depth), BF16),
                pltpu.VMEM((n_zh, few, depth), BF16),
                pltpu.VMEM((n_zh, few, depth), BF16),
                pltpu.VMEM((rows, depth), F32),
                pltpu.VMEM((n_zl, rows, depth), BF16),
                pltpu.VMEM((cols, depth), F32),
                dma((4,)),
                pltpu.SemaphoreType.REGULAR((3,)),
                dma, dma,
                dma((2, n_dp // 2)), dma((n_dp,)),
                dma((n_dp, 2)), dma((n_dp, 2)),
                dma((4,)), dma((4,)),
                dma((2,)), dma((2,)),
                dma((n_dp,)), dma((n_dp,)),
                dma((n_zl,)), dma((n_zl,)),
                dma((n_zh,)), dma((n_zh,)),
                dma, dma,
                dma, dma,
                dma, dma,
                dma((n_dp,)), dma((n_dp,)),
                dma((n_zl,)), dma((n_zl,)),
                dma((n_zh,)), dma((n_zh,)),
                dma((n_zh,)), dma((n_zh,)),
                dma((n_zl,)), dma((n_zl,)),
            ],
            compiler_params=pltpu.CompilerParams(
                collective_id=0, has_side_effects=True, vmem_limit_bytes=56 << 20
            ),
        )(hidden.reshape(4, tok // 4, depth), head_weight.T, teacher_logits.T, response_start)
        kl, grad_hidden, grad_head = pl.pallas_call(
            copy_kernel,
            name="results",
            out_shape=shapes,
            in_specs=[hbm, hbm, hbm],
            out_specs=(hbm, hbm, hbm),
            scratch_shapes=[dma((3,))],
        )(*results)
        return kl.reshape(own), grad_hidden, grad_head.T

    return jax.shard_map(
        per_device,
        mesh=mesh,
        in_specs=(P("dp", "mp"), P("mp", ("dp", "vocab")), P("mp", ("dp", "vocab")), P()),
        out_specs=(P("mp"), P("dp", "mp"), P("mp", ("dp", "vocab"))),
        check_vma=False,
    )
```

```python
import functools

import jax
import jax.numpy as jnp
from jax import lax
from jax.experimental import pallas as pl
from jax.experimental.pallas import tpu as pltpu
from jax.sharding import PartitionSpec as P

LEN = 256
MESH = pl.DeviceIdType.MESH
F32 = jnp.float32
BF16 = jnp.bfloat16

ROW_MS, ROW_SS, ROW_MT, ROW_ST, ROW_C = range(5)


class Group:
    def __init__(self, n, me, device):
        self.n, self.me, self.device = n, me, device

    def others(self):
        return [lax.rem(self.me + k, self.n) for k in range(1, self.n)]

    def copy(self, src, dst, send, recv, to):
        return pltpu.make_async_remote_copy(
            src_ref=src,
            dst_ref=dst,
            send_sem=send,
            recv_sem=recv,
            device_id=self.device(to),
            device_id_type=MESH,
        )


def gather_start(group, src, held, send, recv):
    for peer in group.others():
        group.copy(src, held.at[group.me], send.at[peer], recv.at[group.me], peer).start()


def gather_wait(group, src, held, send, recv):
    for peer in group.others():
        copy = group.copy(src, held.at[peer], send.at[peer], recv.at[peer], peer)
        copy.wait_recv()
        copy.wait_send()


def scatter_start(group, parts, held, send, recv):
    for peer in group.others():
        group.copy(parts.at[peer], held.at[group.me], send.at[peer], recv.at[group.me], peer).start()


def scatter_wait(group, parts, held, send, recv):
    for peer in group.others():
        copy = group.copy(parts.at[peer], held.at[peer], send.at[peer], recv.at[peer], peer)
        copy.wait_recv()
        copy.wait_send()


def merge(held, n):
    rows = [[held[i, r : r + 1, :] for r in range(5)] for i in range(n)]
    top_s = functools.reduce(jnp.maximum, [row[ROW_MS] for row in rows])
    top_t = functools.reduce(jnp.maximum, [row[ROW_MT] for row in rows])
    sum_s = sum_t = cross = None
    for row in rows:
        scale_s = jnp.exp(row[ROW_MS] - top_s)
        scale_t = jnp.exp(row[ROW_MT] - top_t)
        terms = row[ROW_SS] * scale_s, row[ROW_ST] * scale_t, row[ROW_C] * scale_t
        if sum_s is None:
            sum_s, sum_t, cross = terms
        else:
            sum_s, sum_t, cross = sum_s + terms[0], sum_t + terms[1], cross + terms[2]
    return top_s, sum_s, top_t, sum_t, cross


def store_stats(ref, stats):
    for row, value in enumerate(stats):
        ref[row : row + 1, :] = value


def kernel(
    sizes,
    hidden_ref, head_hbm, teacher_hbm, start_ref,
    kl_ref, grad_hidden_ref, grad_head_hbm,
    head_ref, teacher_ref, head_out,
    hid, parts, swap_in, cross_out, cross_in, stud,
    st_dp, st_zl, st_zh, grads, gh_out, gh_in, acc,
    zl_out, zl_in, zh_out, zh_in, fin_h, fin_f, fin_l, head_acc,
    local_sem, ready, hx_s, hx_r, hy_s, hy_r, hz_s, hz_r,
    swap_s, swap_r, cross_s, cross_r,
    sdp_s, sdp_r, szl_s, szl_r, szh_s, szh_r,
    gx_s, gx_r, gc_s, gc_r, gd_s, gd_r, gh_s, gh_r,
    zl_s, zl_r, zh_s, zh_r, fh_s, fh_r, fl_s, fl_r,
):
    n_dp, n_z, n_zl, n_zh = sizes
    n_y = n_dp // 2
    sub, depth = hidden_ref.shape[1:]
    tok = 4 * sub
    d, z, m = lax.axis_index("dp"), lax.axis_index("vocab"), lax.axis_index("mp")
    x, c = m // 2, m % 2
    y = d // 2
    partner = 2 * y + (1 - d % 2)
    zl, zh = z % n_zl, z // n_zl
    other_core, other_chip = 2 * x + (1 - c), 2 * (1 - x) + c
    diagonal = 2 * (1 - x) + (1 - c)
    up, down = lax.rem(z + 1, n_z), lax.rem(z + n_z - 1, n_z)

    dp = Group(n_dp, d, lambda i: (i, z, m))
    column = Group(n_y, y, lambda i: (2 * i + d % 2, z, m))
    ring = Group(n_z, z, lambda i: (d, i, m))
    near = Group(n_zl, zl, lambda i: (d, zh * n_zl + i, m))
    far = Group(n_zh, zh, lambda i: (d, i * n_zl + zl, m))
    mp = Group(4, m, lambda i: (d, z, i))
    far_next = [far.device(lax.rem(zh + k, n_zh)) for k in (1, n_zh - 1)]

    barrier = pltpu.get_barrier_semaphore()
    peers = [g.device(p) for g in (dp, near) for p in g.others()] + far_next
    peers += [mp.device(other_core), mp.device(other_chip), ring.device(up), ring.device(down)]
    for peer in peers:
        pl.semaphore_signal(barrier, inc=1, device_id=peer, device_id_type=MESH)
    own = pltpu.make_async_copy(hidden_ref, hid.at[d], local_sem.at[0])
    own.start()
    load_head = pltpu.make_async_copy(head_hbm, head_ref, local_sem.at[1])
    load_head.start()
    load_teacher = pltpu.make_async_copy(teacher_hbm, teacher_ref, local_sem.at[2])
    load_teacher.start()
    own.wait()
    pl.semaphore_wait(barrier, len(peers))

    def tell(r):
        for peer in far_next:
            pl.semaphore_signal(ready.at[r], inc=1, device_id=peer, device_id_type=MESH)

    def hear(r):
        pl.semaphore_wait(ready.at[r], 2)

    half = pl.ds(2 * (z % 2), 2)

    def to_partner(block):
        part = hid.at[block, half]
        return dp.copy(part, part, hx_s, hx_r, partner)

    def to_column(block, peer):
        part = hid.at[block, half]
        return column.copy(part, part, hy_s.at[block % 2, peer], hy_r.at[block], peer)

    def to_ring(block, side, parity):
        part = hid.at[block, 2 * parity + side]
        return ring.copy(part, part, hz_s.at[block, side], hz_r.at[block, side], (up, down)[side])

    def pass_on(block):
        for side in range(2):
            to_ring(block, side, z % 2).start()

    to_partner(d).start()
    for i in range(2):
        block = 2 * y + i

        @pl.when(block != d)
        def _():
            to_partner(partner).wait_recv()

        for peer in column.others():
            to_column(block, peer).start()
    pass_on(partner)
    if n_zh >= 4:
        tell(0)

    def blocks_of(i):
        return [2 * row + i for row in column.others()]

    def forward(i):
        for block in blocks_of(i):
            to_column(block, block // 2).wait_recv()
            pass_on(block)

    def arrive(i):
        for block in blocks_of(i):
            for side in range(2):
                to_ring(block, side, 1 - z % 2).wait_recv()

        @pl.when(2 * y + i != d)
        def _():
            for side in range(2):
                to_ring(partner, side, 1 - z % 2).wait_recv()

    def swap(k):
        return mp.copy(parts.at[k, 0], swap_in.at[k], swap_s.at[k], swap_r.at[k], other_core)

    def cross(k):
        return mp.copy(cross_out.at[k], cross_in.at[k], cross_s.at[k], cross_r.at[k], other_chip)

    def partial_sums(k):
        chip = (1 - x) if k < 2 else x

        def one(j, carry):
            core = jnp.where(j == 0, 1 - c, c)
            block = hid[2 * (2 * chip + core) + k % 2].reshape(tok, depth)
            parts[k, j] = lax.dot_general(
                head_ref[...], block, (((1,), (1,)), ((), ())), preferred_element_type=F32
            )
            return carry

        lax.fori_loop(0, 2, one, 0)
        swap(k).start()

    def send_cross(k):
        swap(k).wait()
        cross_out[k] = parts[k, 1] + swap_in[k]
        cross(k).start()

    forward(0)
    load_head.wait()
    arrive(0)
    partial_sums(0)
    send_cross(0)
    if n_zh >= 4:
        hear(0)
        tell(1)
    forward(1)
    arrive(1)
    partial_sums(1)
    send_cross(1)
    if n_zh >= 4:
        hear(1)
        tell(2)
    partial_sums(2)
    partial_sums(3)
    load_teacher.wait()

    for h in range(2):
        cols = slice(h * tok, (h + 1) * tok)
        swap(2 + h).wait()
        stud[h] = parts[2 + h, 1] + swap_in[2 + h]
        cross(h).wait()
        s = stud[h] + cross_in[h]
        stud[h] = s
        t = teacher_ref[:, cols].astype(F32)
        top_s = jnp.max(s, axis=0, keepdims=True)
        top_t = jnp.max(t, axis=0, keepdims=True)
        exp_t = jnp.exp(t - top_t)
        stats = (
            top_s,
            jnp.sum(jnp.exp(s - top_s), axis=0, keepdims=True),
            top_t,
            jnp.sum(exp_t, axis=0, keepdims=True),
            jnp.sum(exp_t * (t - s), axis=0, keepdims=True),
        )
        for row, value in enumerate(stats):
            st_dp[d, row : row + 1, cols] = value

    to_partner(d).wait_send()
    for i in range(2):
        for peer in column.others():
            to_column(2 * y + i, peer).wait_send()
    for block in [partner] + blocks_of(0) + blocks_of(1):
        for side in range(2):
            to_ring(block, side, z % 2).wait_send()

    def share(group, held, send, recv):
        gather_start(group, held.at[group.me], held, send, recv)
        gather_wait(group, held.at[group.me], held, send, recv)
        return merge(held, group.n)

    store_stats(st_zl.at[zl], share(dp, st_dp, sdp_s, sdp_r))
    store_stats(st_zh.at[zh], share(near, st_zl, szl_s, szl_r))
    if n_zh >= 4:
        hear(2)
    top_s, sum_s, top_t, sum_t, cross_term = share(far, st_zh, szh_s, szh_r)
    position = lax.broadcasted_iota(jnp.int32, (1, 2 * tok), 1)
    mask = jnp.where(position >= start_ref[m], 1.0, 0.0).astype(F32)
    scale_s, scale_t = mask / sum_s, mask / sum_t

    def grad_x():
        return mp.copy(grads.at[m], grads.at[m], gx_s, gx_r, other_chip)

    def grad_c():
        return mp.copy(grads.at[m], grads.at[m], gc_s, gc_r, other_core)

    def grad_d():
        return mp.copy(grads.at[other_chip], grads.at[other_chip], gd_s, gd_r, other_core)

    for h in range(2):
        cols = slice(h * tok, (h + 1) * tok)
        exp_s = jnp.exp(stud[h] - top_s[:, cols])
        exp_t = jnp.exp(teacher_ref[:, cols].astype(F32) - top_t[:, cols])
        grads[m, :, cols] = (exp_s * scale_s[:, cols] - exp_t * scale_t[:, cols]).astype(BF16)
    grad_x().start()
    grad_c().start()
    kl_ref[...] = mask * (cross_term / sum_t - top_t - jnp.log(sum_t) + top_s + jnp.log(sum_s))

    def owner_copy(block):
        return dp.copy(gh_out.at[block], gh_in.at[d], gh_s.at[block], gh_r.at[d], block)

    def hidden_terms(quarter):
        for h in range(2):
            block = 2 * quarter + h
            gh_out[block] = lax.dot_general(
                grads[quarter, :, h * tok : (h + 1) * tok],
                head_ref[...],
                (((0,), (0,)), ((), ())),
                preferred_element_type=F32,
            ).astype(BF16)

            @pl.when(block != d)
            def _():
                owner_copy(block).start()

    hidden_terms(m)
    grad_c().wait()
    hidden_terms(other_core)
    grad_x().wait()
    grad_d().start()
    hidden_terms(other_chip)
    grad_d().wait()
    hidden_terms(diagonal)

    scatter_wait(dp, gh_out, gh_in, gh_s, gh_r)
    gh_in[d] = gh_out[d]
    total = gh_in[0].astype(F32)
    for i in range(1, n_dp):
        total = total + gh_in[i].astype(F32)

    rows = tok // n_zl
    for i in range(n_zl):
        acc[i] = total[i * rows : (i + 1) * rows, :]
        zl_out[i] = acc[i].astype(BF16)
    scatter_start(near, zl_out, zl_in, zl_s, zl_r)
    scatter_wait(near, zl_out, zl_in, zl_s, zl_r)
    total = acc[zl]
    for peer in near.others():
        total = total + zl_in[peer].astype(F32)
    few = rows // n_zh
    for i in range(n_zh):
        zh_out[i] = total[i * few : (i + 1) * few, :].astype(BF16)
    scatter_start(far, zh_out, zh_in, zh_s, zh_r)

    def head_step(quarter, carry):
        tokens = hid[pl.ds(2 * quarter, 2)].reshape(2 * tok, depth)
        head_acc[...] += jnp.dot(grads[quarter], tokens, preferred_element_type=F32)
        return carry

    head_acc[...] = jnp.zeros_like(head_acc)
    lax.fori_loop(0, n_y, head_step, 0)
    head_out[...] = head_acc[...].astype(BF16)
    store_head = pltpu.make_async_copy(head_out, grad_head_hbm, local_sem.at[3])
    store_head.start()

    scatter_wait(far, zh_out, zh_in, zh_s, zh_r)
    zh_in[zh] = zh_out[zh]
    total = zh_in[0].astype(F32)
    for i in range(1, n_zh):
        total = total + zh_in[i].astype(F32)
    fin_h[zh] = total.astype(BF16)
    gather_start(far, fin_h.at[zh], fin_h, fh_s, fh_r)
    gather_wait(far, fin_h.at[zh], fin_h, fh_s, fh_r)
    for i in range(n_zh):
        fin_f[i * few : (i + 1) * few, :] = fin_h[i].astype(F32)
    fin_l[zl] = fin_f[...].astype(BF16)
    gather_start(near, fin_l.at[zl], fin_l, fl_s, fl_r)
    gather_wait(near, fin_l.at[zl], fin_l, fl_s, fl_r)
    for i in range(n_zl):
        grad_hidden_ref[i * rows : (i + 1) * rows, :] = fin_l[i].astype(F32)

    store_head.wait()


def copy_kernel(*refs):
    sources, results, held, (load, store) = refs[:3], refs[3:6], refs[6:9], refs[9:]
    loads = [pltpu.make_async_copy(a, b, load.at[i]) for i, (a, b) in enumerate(zip(sources, held))]
    stores = [pltpu.make_async_copy(a, b, store.at[i]) for i, (a, b) in enumerate(zip(held, results))]
    for copy in loads:
        copy.start()
    for before, after in zip(loads, stores):
        before.wait()
        after.start()
    for copy in stores:
        copy.wait()


def solution(mesh):
    n_dp, n_z, n_mp = mesh.shape["dp"], mesh.shape["vocab"], mesh.shape["mp"]
    n_zl = min(4, n_z)
    n_zh = n_z // n_zl

    def per_device(hidden, head_weight, teacher_logits, response_start):
        tok, depth = hidden.shape
        own, cols = teacher_logits.shape
        assert n_mp == 4 and own == 2 * tok == LEN and n_dp == 8 and n_zh == 8
        rows = tok // n_zl
        few = rows // n_zh
        dma = pltpu.SemaphoreType.DMA
        vmem = pl.BlockSpec(memory_space=pltpu.VMEM)
        hbm = pl.BlockSpec(memory_space=pl.ANY)
        shapes = (
            jax.ShapeDtypeStruct((1, own), F32),
            jax.ShapeDtypeStruct((tok, depth), F32),
            jax.ShapeDtypeStruct((cols, depth), BF16),
        )
        results = pl.pallas_call(
            functools.partial(kernel, (n_dp, n_z, n_zl, n_zh)),
            name="distill",
            out_shape=shapes,
            in_specs=[hbm, hbm, hbm, pl.BlockSpec(memory_space=pltpu.SMEM)],
            out_specs=(vmem, vmem, hbm),
            scratch_shapes=[
                pltpu.VMEM((cols, depth), BF16),
                pltpu.VMEM((cols, own), BF16),
                pltpu.VMEM((cols, depth), BF16),
                pltpu.VMEM((n_dp, 4, tok // 4, depth), BF16),
                pltpu.VMEM((4, 2, cols, tok), F32),
                pltpu.VMEM((4, cols, tok), F32),
                pltpu.VMEM((2, cols, tok), F32),
                pltpu.VMEM((2, cols, tok), F32),
                pltpu.VMEM((2, cols, tok), F32),
                pltpu.VMEM((n_dp, 8, own), F32),
                pltpu.VMEM((n_zl, 8, own), F32),
                pltpu.VMEM((n_zh, 8, own), F32),
                pltpu.VMEM((4, cols, own), BF16),
                pltpu.VMEM((n_dp, tok, depth), BF16),
                pltpu.VMEM((n_dp, tok, depth), BF16),
                pltpu.VMEM((n_zl, rows, depth), F32),
                pltpu.VMEM((n_zl, rows, depth), BF16),
                pltpu.VMEM((n_zl, rows, depth), BF16),
                pltpu.VMEM((n_zh, few, depth), BF16),
                pltpu.VMEM((n_zh, few, depth), BF16),
                pltpu.VMEM((n_zh, few, depth), BF16),
                pltpu.VMEM((rows, depth), F32),
                pltpu.VMEM((n_zl, rows, depth), BF16),
                pltpu.VMEM((cols, depth), F32),
                dma((4,)),
                pltpu.SemaphoreType.REGULAR((3,)),
                dma, dma,
                dma((2, n_dp // 2)), dma((n_dp,)),
                dma((n_dp, 2)), dma((n_dp, 2)),
                dma((4,)), dma((4,)),
                dma((2,)), dma((2,)),
                dma((n_dp,)), dma((n_dp,)),
                dma((n_zl,)), dma((n_zl,)),
                dma((n_zh,)), dma((n_zh,)),
                dma, dma,
                dma, dma,
                dma, dma,
                dma((n_dp,)), dma((n_dp,)),
                dma((n_zl,)), dma((n_zl,)),
                dma((n_zh,)), dma((n_zh,)),
                dma((n_zh,)), dma((n_zh,)),
                dma((n_zl,)), dma((n_zl,)),
            ],
            compiler_params=pltpu.CompilerParams(
                collective_id=0, has_side_effects=True, vmem_limit_bytes=56 << 20
            ),
        )(hidden.reshape(4, tok // 4, depth), head_weight.T, teacher_logits.T, response_start)
        kl, grad_hidden, grad_head = pl.pallas_call(
            copy_kernel,
            name="results",
            out_shape=shapes,
            in_specs=[hbm, hbm, hbm],
            out_specs=(hbm, hbm, hbm),
            scratch_shapes=[pltpu.VMEM(s.shape, s.dtype) for s in shapes] + [dma((3,)), dma((3,))],
        )(*results)
        return kl.reshape(own), grad_hidden, grad_head.T

    return jax.shard_map(
        per_device,
        mesh=mesh,
        in_specs=(P("dp", "mp"), P("mp", ("dp", "vocab")), P("mp", ("dp", "vocab")), P()),
        out_specs=(P("mp"), P("dp", "mp"), P("mp", ("dp", "vocab"))),
        check_vma=False,
    )
```

```python
import functools

import jax
import jax.numpy as jnp
from jax import lax
from jax.experimental import pallas as pl
from jax.experimental.pallas import tpu as pltpu
from jax.sharding import PartitionSpec as P

LEN = 256
MESH = pl.DeviceIdType.MESH
F32 = jnp.float32
BF16 = jnp.bfloat16

ROW_MS, ROW_SS, ROW_MT, ROW_ST, ROW_C = range(5)


class Group:
    def __init__(self, n, me, device):
        self.n, self.me, self.device = n, me, device

    def others(self):
        return [lax.rem(self.me + k, self.n) for k in range(1, self.n)]

    def copy(self, src, dst, send, recv, to):
        return pltpu.make_async_remote_copy(
            src_ref=src,
            dst_ref=dst,
            send_sem=send,
            recv_sem=recv,
            device_id=self.device(to),
            device_id_type=MESH,
        )


def gather_start(group, src, held, send, recv):
    for peer in group.others():
        group.copy(src, held.at[group.me], send.at[peer], recv.at[group.me], peer).start()


def gather_wait(group, src, held, send, recv):
    for peer in group.others():
        copy = group.copy(src, held.at[peer], send.at[peer], recv.at[peer], peer)
        copy.wait_recv()
        copy.wait_send()


def scatter_start(group, parts, held, send, recv):
    for peer in group.others():
        group.copy(parts.at[peer], held.at[group.me], send.at[peer], recv.at[group.me], peer).start()


def scatter_wait(group, parts, held, send, recv):
    for peer in group.others():
        copy = group.copy(parts.at[peer], held.at[peer], send.at[peer], recv.at[peer], peer)
        copy.wait_recv()
        copy.wait_send()


def merge(held, n):
    rows = [[held[i, r : r + 1, :] for r in range(5)] for i in range(n)]
    top_s = functools.reduce(jnp.maximum, [row[ROW_MS] for row in rows])
    top_t = functools.reduce(jnp.maximum, [row[ROW_MT] for row in rows])
    sum_s = sum_t = cross = None
    for row in rows:
        scale_s = jnp.exp(row[ROW_MS] - top_s)
        scale_t = jnp.exp(row[ROW_MT] - top_t)
        terms = row[ROW_SS] * scale_s, row[ROW_ST] * scale_t, row[ROW_C] * scale_t
        if sum_s is None:
            sum_s, sum_t, cross = terms
        else:
            sum_s, sum_t, cross = sum_s + terms[0], sum_t + terms[1], cross + terms[2]
    return top_s, sum_s, top_t, sum_t, cross


def store_stats(ref, stats):
    for row, value in enumerate(stats):
        ref[row : row + 1, :] = value


def kernel(
    sizes,
    hidden_ref, head_hbm, teacher_hbm, start_ref,
    kl_ref, grad_hidden_ref, grad_head_hbm,
    head_ref, teacher_ref, head_out,
    hid, parts, swap_in, cross_out, cross_in, stud,
    st_dp, st_zl, st_zh, grads, gh_out, gz_in, gh_mid, gh_in,
    pair_out, pair_in, zh_out, zh_in, fin_h, fin_f, fin_l, head_acc,
    local_sem, ready, hx_s, hx_r, hy_s, hy_r, hz_s, hz_r,
    swap_s, swap_r, cross_s, cross_r,
    sdp_s, sdp_r, szl_s, szl_r, szh_s, szh_r,
    gx_s, gx_r, gc_s, gc_r, gd_s, gd_r, gz_s, gz_r, gh_s, gh_r,
    pair_s, pair_r, zh_s, zh_r, fh_s, fh_r, fl_s, fl_r,
):
    n_dp, n_z, n_zl, n_zh = sizes
    n_y = n_dp // 2
    sub, depth = hidden_ref.shape[1:]
    tok = 4 * sub
    d, z, m = lax.axis_index("dp"), lax.axis_index("vocab"), lax.axis_index("mp")
    x, c = m // 2, m % 2
    y = d // 2
    partner = 2 * y + (1 - d % 2)
    zl, zh = z % n_zl, z // n_zl
    other_core, other_chip = 2 * x + (1 - c), 2 * (1 - x) + c
    diagonal = 2 * (1 - x) + (1 - c)
    parity = z % 2
    up, down = lax.rem(z + 1, n_z), lax.rem(z + n_z - 1, n_z)

    dp = Group(n_dp, d, lambda i: (i, z, m))
    column = Group(n_y, y, lambda i: (2 * i + d % 2, z, m))
    ring = Group(n_z, z, lambda i: (d, i, m))
    mine = 2 * (zl % 2) + zl // 2
    near = Group(n_zl, mine, lambda i: (d, zh * n_zl + 2 * (i % 2) + i // 2, m))
    far = Group(n_zh, zh, lambda i: (d, i * n_zl + zl, m))
    mp = Group(4, m, lambda i: (d, z, i))
    far_next = [far.device(lax.rem(zh + k, n_zh)) for k in (1, n_zh - 1)]

    barrier = pltpu.get_barrier_semaphore()
    peers = [g.device(p) for g in (dp, near) for p in g.others()] + far_next
    peers += [mp.device(other_core), mp.device(other_chip), ring.device(up), ring.device(down)]
    for peer in peers:
        pl.semaphore_signal(barrier, inc=1, device_id=peer, device_id_type=MESH)
    own = pltpu.make_async_copy(hidden_ref, hid.at[d], local_sem.at[0])
    own.start()
    load_head = pltpu.make_async_copy(head_hbm, head_ref, local_sem.at[1])
    load_head.start()
    load_teacher = pltpu.make_async_copy(teacher_hbm, teacher_ref, local_sem.at[2])
    load_teacher.start()
    own.wait()
    pl.semaphore_wait(barrier, len(peers))

    def tell(r):
        for peer in far_next:
            pl.semaphore_signal(ready.at[r], inc=1, device_id=peer, device_id_type=MESH)

    def hear(r):
        pl.semaphore_wait(ready.at[r], 2)

    half = pl.ds(2 * (z % 2), 2)

    def to_partner(block):
        part = hid.at[block, half]
        return dp.copy(part, part, hx_s, hx_r, partner)

    def to_column(block, peer):
        part = hid.at[block, half]
        return column.copy(part, part, hy_s.at[block % 2, peer], hy_r.at[block], peer)

    def to_ring(block, side, parity):
        part = hid.at[block, 2 * parity + side]
        return ring.copy(part, part, hz_s.at[block, side], hz_r.at[block, side], (up, down)[side])

    def pass_on(block):
        for side in range(2):
            to_ring(block, side, z % 2).start()

    to_partner(d).start()
    for i in range(2):
        block = 2 * y + i

        @pl.when(block != d)
        def _():
            to_partner(partner).wait_recv()

        for peer in column.others():
            to_column(block, peer).start()
    pass_on(partner)
    if n_zh >= 4:
        tell(0)

    def blocks_of(i):
        return [2 * row + i for row in column.others()]

    def forward(i):
        for block in blocks_of(i):
            to_column(block, block // 2).wait_recv()
            pass_on(block)

    def arrive(i):
        for block in blocks_of(i):
            for side in range(2):
                to_ring(block, side, 1 - z % 2).wait_recv()

        @pl.when(2 * y + i != d)
        def _():
            for side in range(2):
                to_ring(partner, side, 1 - z % 2).wait_recv()

    def swap(k):
        return mp.copy(parts.at[k, 0], swap_in.at[k], swap_s.at[k], swap_r.at[k], other_core)

    def cross(k):
        return mp.copy(cross_out.at[k], cross_in.at[k], cross_s.at[k], cross_r.at[k], other_chip)

    def partial_sums(k):
        chip = (1 - x) if k < 2 else x

        def one(j, carry):
            core = jnp.where(j == 0, 1 - c, c)
            block = hid[2 * (2 * chip + core) + k % 2].reshape(tok, depth)
            parts[k, j] = lax.dot_general(
                head_ref[...], block, (((1,), (1,)), ((), ())), preferred_element_type=F32
            )
            return carry

        lax.fori_loop(0, 2, one, 0)
        swap(k).start()

    def send_cross(k):
        swap(k).wait()
        cross_out[k] = parts[k, 1] + swap_in[k]
        cross(k).start()

    forward(0)
    load_head.wait()
    arrive(0)
    partial_sums(0)
    send_cross(0)
    if n_zh >= 4:
        hear(0)
        tell(1)
    forward(1)
    arrive(1)
    partial_sums(1)
    send_cross(1)
    if n_zh >= 4:
        hear(1)
        tell(2)
    partial_sums(2)
    partial_sums(3)
    load_teacher.wait()

    for h in range(2):
        cols = slice(h * tok, (h + 1) * tok)
        swap(2 + h).wait()
        stud[h] = parts[2 + h, 1] + swap_in[2 + h]
        cross(h).wait()
        s = stud[h] + cross_in[h]
        stud[h] = s
        t = teacher_ref[:, cols].astype(F32)
        top_s = jnp.max(s, axis=0, keepdims=True)
        top_t = jnp.max(t, axis=0, keepdims=True)
        exp_t = jnp.exp(t - top_t)
        stats = (
            top_s,
            jnp.sum(jnp.exp(s - top_s), axis=0, keepdims=True),
            top_t,
            jnp.sum(exp_t, axis=0, keepdims=True),
            jnp.sum(exp_t * (t - s), axis=0, keepdims=True),
        )
        for row, value in enumerate(stats):
            st_dp[d, row : row + 1, cols] = value

    to_partner(d).wait_send()
    for i in range(2):
        for peer in column.others():
            to_column(2 * y + i, peer).wait_send()
    for block in [partner] + blocks_of(0) + blocks_of(1):
        for side in range(2):
            to_ring(block, side, z % 2).wait_send()

    def share(group, held, send, recv):
        gather_start(group, held.at[group.me], held, send, recv)
        gather_wait(group, held.at[group.me], held, send, recv)
        return merge(held, group.n)

    store_stats(st_zl.at[mine], share(dp, st_dp, sdp_s, sdp_r))
    store_stats(st_zh.at[zh], share(near, st_zl, szl_s, szl_r))
    if n_zh >= 4:
        hear(2)
    top_s, sum_s, top_t, sum_t, cross_term = share(far, st_zh, szh_s, szh_r)
    position = lax.broadcasted_iota(jnp.int32, (1, 2 * tok), 1)
    mask = jnp.where(position >= start_ref[m], 1.0, 0.0).astype(F32)
    scale_s, scale_t = mask / sum_s, mask / sum_t

    def grad_x(h):
        block = grads.at[2 * m + h]
        return mp.copy(block, block, gx_s.at[h], gx_r.at[h], other_chip)

    def grad_c(h):
        block = grads.at[2 * m + h]
        return mp.copy(block, block, gc_s.at[h], gc_r.at[h], other_core)

    def grad_d(h):
        block = grads.at[2 * other_chip + h]
        return mp.copy(block, block, gd_s.at[h], gd_r.at[h], other_core)

    for h in range(2):
        cols = slice(h * tok, (h + 1) * tok)
        exp_s = jnp.exp(stud[h] - top_s[:, cols])
        exp_t = jnp.exp(teacher_ref[:, cols].astype(F32) - top_t[:, cols])
        grads[2 * m + h] = (exp_s * scale_s[:, cols] - exp_t * scale_t[:, cols]).astype(BF16)
        grad_x(h).start()
        grad_c(h).start()
    kl_ref[...] = mask * (cross_term / sum_t - top_t - jnp.log(sum_t) + top_s + jnp.log(sum_s))

    def to_neighbour(block, side):
        return ring.copy(
            gh_out.at[block, 2 * (1 - parity) + side],
            gz_in.at[block, side],
            gz_s.at[block, side],
            gz_r.at[block, side],
            (up, down)[side],
        )

    def owner_copy(block):
        return dp.copy(gh_mid.at[block], gh_in.at[d], gh_s.at[block], gh_r.at[d], block)

    def hidden_terms(block):
        gh_out[block] = (
            lax.dot_general(
                grads[block], head_ref[...], (((0,), (0,)), ((), ())), preferred_element_type=F32
            )
            .astype(BF16)
            .reshape(4, sub, depth)
        )
        for side in range(2):
            to_neighbour(block, side).start()

    def hand_over(block):
        for side in range(2):
            to_neighbour(block, side).wait()
            own_rows = gh_out[block, 2 * parity + side].astype(F32)
            gh_mid[block, side] = (own_rows + gz_in[block, side].astype(F32)).astype(BF16)

        @pl.when(block != d)
        def _():
            owner_copy(block).start()

    for h in range(2):
        hidden_terms(2 * m + h)
    for h in range(2):
        grad_c(h).wait()
        hidden_terms(2 * other_core + h)
    for h in range(2):
        hand_over(2 * m + h)
    for h in range(2):
        grad_x(h).wait()
        grad_d(h).start()
        hidden_terms(2 * other_chip + h)
        hand_over(2 * other_core + h)
    for h in range(2):
        grad_d(h).wait()
        hidden_terms(2 * diagonal + h)
    for h in range(2):
        hand_over(2 * other_chip + h)
    for h in range(2):
        hand_over(2 * diagonal + h)

    scatter_wait(dp, gh_mid, gh_in, gh_s, gh_r)
    gh_in[d] = gh_mid[d]
    rows = tok // n_zl

    def pair_copy():
        return near.copy(pair_out, pair_in, pair_s, pair_r, 2 * (mine // 2) + 1 - mine % 2)

    def plane_sum(side):
        total = gh_in[0, side].astype(F32)
        for i in range(1, n_dp):
            total = total + gh_in[i, side].astype(F32)
        return total

    pair_out[...] = plane_sum(1 - mine % 2).astype(BF16)
    pair_copy().start()
    total = plane_sum(mine % 2)
    pair_copy().wait()
    total = total + pair_in[...].astype(F32)
    few = rows // n_zh
    for i in range(n_zh):
        zh_out[i] = total[i * few : (i + 1) * few, :].astype(BF16)
    scatter_start(far, zh_out, zh_in, zh_s, zh_r)

    def head_step(block, carry):
        tokens = hid[block].reshape(tok, depth)
        head_acc[...] += jnp.dot(grads[block], tokens, preferred_element_type=F32)
        return carry

    head_acc[...] = jnp.zeros_like(head_acc)
    lax.fori_loop(0, n_dp, head_step, 0)
    head_out[...] = head_acc[...].astype(BF16)
    store_head = pltpu.make_async_copy(head_out, grad_head_hbm, local_sem.at[3])
    store_head.start()

    scatter_wait(far, zh_out, zh_in, zh_s, zh_r)
    zh_in[zh] = zh_out[zh]
    total = zh_in[0].astype(F32)
    for i in range(1, n_zh):
        total = total + zh_in[i].astype(F32)
    fin_h[zh] = total.astype(BF16)
    gather_start(far, fin_h.at[zh], fin_h, fh_s, fh_r)
    gather_wait(far, fin_h.at[zh], fin_h, fh_s, fh_r)
    for i in range(n_zh):
        fin_f[i * few : (i + 1) * few, :] = fin_h[i].astype(F32)
    fin_l[mine] = fin_f[...].astype(BF16)
    gather_start(near, fin_l.at[mine], fin_l, fl_s, fl_r)
    gather_wait(near, fin_l.at[mine], fin_l, fl_s, fl_r)
    for i in range(n_zl):
        grad_hidden_ref[i * rows : (i + 1) * rows, :] = fin_l[i].astype(F32)

    store_head.wait()


def copy_kernel(*refs):
    sources, results, held, (load, store) = refs[:3], refs[3:6], refs[6:9], refs[9:]
    loads = [pltpu.make_async_copy(a, b, load.at[i]) for i, (a, b) in enumerate(zip(sources, held))]
    stores = [pltpu.make_async_copy(a, b, store.at[i]) for i, (a, b) in enumerate(zip(held, results))]
    for copy in loads:
        copy.start()
    for before, after in zip(loads, stores):
        before.wait()
        after.start()
    for copy in stores:
        copy.wait()


def solution(mesh):
    n_dp, n_z, n_mp = mesh.shape["dp"], mesh.shape["vocab"], mesh.shape["mp"]
    n_zl = min(4, n_z)
    n_zh = n_z // n_zl

    def per_device(hidden, head_weight, teacher_logits, response_start):
        tok, depth = hidden.shape
        own, cols = teacher_logits.shape
        assert n_mp == 4 and own == 2 * tok == LEN and n_dp == 8 and n_zl == 4 and n_zh == 8
        rows = tok // n_zl
        few = rows // n_zh
        dma = pltpu.SemaphoreType.DMA
        vmem = pl.BlockSpec(memory_space=pltpu.VMEM)
        hbm = pl.BlockSpec(memory_space=pl.ANY)
        shapes = (
            jax.ShapeDtypeStruct((1, own), F32),
            jax.ShapeDtypeStruct((tok, depth), F32),
            jax.ShapeDtypeStruct((cols, depth), BF16),
        )
        results = pl.pallas_call(
            functools.partial(kernel, (n_dp, n_z, n_zl, n_zh)),
            name="distill",
            out_shape=shapes,
            in_specs=[hbm, hbm, hbm, pl.BlockSpec(memory_space=pltpu.SMEM)],
            out_specs=(vmem, vmem, hbm),
            scratch_shapes=[
                pltpu.VMEM((cols, depth), BF16),
                pltpu.VMEM((cols, own), BF16),
                pltpu.VMEM((cols, depth), BF16),
                pltpu.VMEM((n_dp, 4, tok // 4, depth), BF16),
                pltpu.VMEM((4, 2, cols, tok), F32),
                pltpu.VMEM((4, cols, tok), F32),
                pltpu.VMEM((2, cols, tok), F32),
                pltpu.VMEM((2, cols, tok), F32),
                pltpu.VMEM((2, cols, tok), F32),
                pltpu.VMEM((n_dp, 8, own), F32),
                pltpu.VMEM((n_zl, 8, own), F32),
                pltpu.VMEM((n_zh, 8, own), F32),
                pltpu.VMEM((n_dp, cols, tok), BF16),
                pltpu.VMEM((n_dp, 4, tok // 4, depth), BF16),
                pltpu.VMEM((n_dp, 2, tok // 4, depth), BF16),
                pltpu.VMEM((n_dp, 2, tok // 4, depth), BF16),
                pltpu.VMEM((n_dp, 2, tok // 4, depth), BF16),
                pltpu.VMEM((rows, depth), BF16),
                pltpu.VMEM((rows, depth), BF16),
                pltpu.VMEM((n_zh, few, depth), BF16),
                pltpu.VMEM((n_zh, few, depth), BF16),
                pltpu.VMEM((n_zh, few, depth), BF16),
                pltpu.VMEM((rows, depth), F32),
                pltpu.VMEM((n_zl, rows, depth), BF16),
                pltpu.VMEM((cols, depth), F32),
                dma((4,)),
                pltpu.SemaphoreType.REGULAR((3,)),
                dma, dma,
                dma((2, n_dp // 2)), dma((n_dp,)),
                dma((n_dp, 2)), dma((n_dp, 2)),
                dma((4,)), dma((4,)),
                dma((2,)), dma((2,)),
                dma((n_dp,)), dma((n_dp,)),
                dma((n_zl,)), dma((n_zl,)),
                dma((n_zh,)), dma((n_zh,)),
                dma((2,)), dma((2,)),
                dma((2,)), dma((2,)),
                dma((2,)), dma((2,)),
                dma((n_dp, 2)), dma((n_dp, 2)),
                dma((n_dp,)), dma((n_dp,)),
                dma, dma,
                dma((n_zh,)), dma((n_zh,)),
                dma((n_zh,)), dma((n_zh,)),
                dma((n_zl,)), dma((n_zl,)),
            ],
            compiler_params=pltpu.CompilerParams(
                collective_id=0, has_side_effects=True, vmem_limit_bytes=56 << 20
            ),
        )(hidden.reshape(4, tok // 4, depth), head_weight.T, teacher_logits.T, response_start)
        kl, grad_hidden, grad_head = pl.pallas_call(
            copy_kernel,
            name="results",
            out_shape=shapes,
            in_specs=[hbm, hbm, hbm],
            out_specs=(hbm, hbm, hbm),
            scratch_shapes=[pltpu.VMEM(s.shape, s.dtype) for s in shapes] + [dma((3,)), dma((3,))],
        )(*results)
        return kl.reshape(own), grad_hidden, grad_head.T

    return jax.shard_map(
        per_device,
        mesh=mesh,
        in_specs=(P("dp", "mp"), P("mp", ("dp", "vocab")), P("mp", ("dp", "vocab")), P()),
        out_specs=(P("mp"), P("dp", "mp"), P("mp", ("dp", "vocab"))),
        check_vma=False,
    )
```

```python
import functools

import jax
import jax.numpy as jnp
from jax import lax
from jax.experimental import pallas as pl
from jax.experimental.pallas import tpu as pltpu
from jax.sharding import PartitionSpec as P

LEN = 256
MESH = pl.DeviceIdType.MESH
F32 = jnp.float32
BF16 = jnp.bfloat16

ROW_MS, ROW_SS, ROW_MT, ROW_ST, ROW_C = range(5)


class Group:
    def __init__(self, n, me, device):
        self.n, self.me, self.device = n, me, device

    def others(self):
        shifts = sorted(range(1, self.n), key=lambda k: -min(k, self.n - k))
        return [lax.rem(self.me + k, self.n) for k in shifts]

    def copy(self, src, dst, send, recv, to):
        return pltpu.make_async_remote_copy(
            src_ref=src,
            dst_ref=dst,
            send_sem=send,
            recv_sem=recv,
            device_id=self.device(to),
            device_id_type=MESH,
        )


def gather_start(group, src, held, send, recv):
    for peer in group.others():
        group.copy(src, held.at[group.me], send.at[peer], recv.at[group.me], peer).start()


def gather_wait(group, src, held, send, recv):
    for peer in group.others():
        copy = group.copy(src, held.at[peer], send.at[peer], recv.at[peer], peer)
        copy.wait_recv()
        copy.wait_send()


def scatter_start(group, parts, held, send, recv):
    for peer in group.others():
        group.copy(parts.at[peer], held.at[group.me], send.at[peer], recv.at[group.me], peer).start()


def scatter_wait(group, parts, held, send, recv):
    for peer in group.others():
        copy = group.copy(parts.at[peer], held.at[peer], send.at[peer], recv.at[peer], peer)
        copy.wait_recv()
        copy.wait_send()


def merge(held, n):
    rows = [[held[i, r : r + 1, :] for r in range(5)] for i in range(n)]
    top_s = functools.reduce(jnp.maximum, [row[ROW_MS] for row in rows])
    top_t = functools.reduce(jnp.maximum, [row[ROW_MT] for row in rows])
    sum_s = sum_t = cross = None
    for row in rows:
        scale_s = jnp.exp(row[ROW_MS] - top_s)
        scale_t = jnp.exp(row[ROW_MT] - top_t)
        terms = row[ROW_SS] * scale_s, row[ROW_ST] * scale_t, row[ROW_C] * scale_t
        if sum_s is None:
            sum_s, sum_t, cross = terms
        else:
            sum_s, sum_t, cross = sum_s + terms[0], sum_t + terms[1], cross + terms[2]
    return top_s, sum_s, top_t, sum_t, cross


def store_stats(ref, stats):
    for row, value in enumerate(stats):
        ref[row : row + 1, :] = value


def kernel(
    sizes,
    hidden_ref, head_hbm, teacher_hbm, start_ref,
    kl_ref, grad_hidden_ref, grad_head_hbm,
    head_ref, teacher_ref, head_out,
    hid, parts, swap_in, cross_out, cross_in, stud,
    st_dp, st_zl, st_zh, grads, gh_out, gz_in, gh_mid, gh_in,
    zs_out, zs_in, fin, fin_other, head_acc,
    local_sem, ready, hx_s, hx_r, hy_s, hy_r, hz_s, hz_r,
    swap_s, swap_r, cross_s, cross_r,
    sdp_s, sdp_r, szl_s, szl_r, szh_s, szh_r,
    gx_s, gx_r, gc_s, gc_r, gd_s, gd_r, gz_s, gz_r, gh_s, gh_r,
    zs_s, zs_r, fa_s, fa_r, fo_s, fo_r,
):
    n_dp, n_z, n_zl, n_zh = sizes
    n_y = n_dp // 2
    sub, depth = hidden_ref.shape[1:]
    tok = 4 * sub
    d, z, m = lax.axis_index("dp"), lax.axis_index("vocab"), lax.axis_index("mp")
    x, c = m // 2, m % 2
    y = d // 2
    partner = 2 * y + (1 - d % 2)
    zl, zh = z % n_zl, z // n_zl
    other_core, other_chip = 2 * x + (1 - c), 2 * (1 - x) + c
    diagonal = 2 * (1 - x) + (1 - c)
    parity = z % 2
    up, down = lax.rem(z + 1, n_z), lax.rem(z + n_z - 1, n_z)

    dp = Group(n_dp, d, lambda i: (i, z, m))
    column = Group(n_y, y, lambda i: (2 * i + d % 2, z, m))
    ring = Group(n_z, z, lambda i: (d, i, m))
    mine = 2 * (zl % 2) + zl // 2
    near = Group(n_zl, mine, lambda i: (d, zh * n_zl + 2 * (i % 2) + i // 2, m))
    alike = Group(n_z // 2, z // 2, lambda i: (d, 2 * i + parity, m))
    far = Group(n_zh, zh, lambda i: (d, i * n_zl + zl, m))
    mp = Group(4, m, lambda i: (d, z, i))
    far_next = [far.device(lax.rem(zh + k, n_zh)) for k in (1, n_zh - 1)]

    barrier = pltpu.get_barrier_semaphore()
    peers = [g.device(p) for g in (dp, near) for p in g.others()] + far_next
    peers += [mp.device(other_core), mp.device(other_chip), ring.device(up), ring.device(down)]
    peers += [ring.device(lax.rem(z + k, n_z)) for k in (2, n_z - 2)]
    for peer in peers:
        pl.semaphore_signal(barrier, inc=1, device_id=peer, device_id_type=MESH)
    own = pltpu.make_async_copy(hidden_ref, hid.at[d], local_sem.at[0])
    own.start()
    load_head = pltpu.make_async_copy(head_hbm, head_ref, local_sem.at[1])
    load_head.start()
    load_teacher = pltpu.make_async_copy(teacher_hbm, teacher_ref, local_sem.at[2])
    load_teacher.start()
    own.wait()
    pl.semaphore_wait(barrier, len(peers))

    def tell(r):
        for peer in far_next:
            pl.semaphore_signal(ready.at[r], inc=1, device_id=peer, device_id_type=MESH)

    def hear(r):
        pl.semaphore_wait(ready.at[r], 2)

    half = pl.ds(2 * (z % 2), 2)

    def to_partner(block):
        part = hid.at[block, half]
        return dp.copy(part, part, hx_s, hx_r, partner)

    def to_column(block, peer):
        part = hid.at[block, half]
        return column.copy(part, part, hy_s.at[block % 2, peer], hy_r.at[block], peer)

    def to_ring(block, side, parity):
        part = hid.at[block, 2 * parity + side]
        return ring.copy(part, part, hz_s.at[block, side], hz_r.at[block, side], (up, down)[side])

    def pass_on(block):
        for side in range(2):
            to_ring(block, side, z % 2).start()

    to_partner(d).start()
    for i in range(2):
        block = 2 * y + i

        @pl.when(block != d)
        def _():
            to_partner(partner).wait_recv()

        for peer in column.others():
            to_column(block, peer).start()
    pass_on(partner)
    if n_zh >= 4:
        tell(0)

    def blocks_of(i):
        return [2 * row + i for row in reversed(column.others())]

    def forward(i):
        for block in blocks_of(i):
            to_column(block, block // 2).wait_recv()
            pass_on(block)

    def arrive(i):
        for block in blocks_of(i):
            for side in range(2):
                to_ring(block, side, 1 - z % 2).wait_recv()

        @pl.when(2 * y + i != d)
        def _():
            for side in range(2):
                to_ring(partner, side, 1 - z % 2).wait_recv()

    def swap(k):
        return mp.copy(parts.at[k, 0], swap_in.at[k], swap_s.at[k], swap_r.at[k], other_core)

    def cross(k):
        return mp.copy(cross_out.at[k], cross_in.at[k], cross_s.at[k], cross_r.at[k], other_chip)

    def partial_sums(k):
        chip = (1 - x) if k < 2 else x

        def one(j, carry):
            core = jnp.where(j == 0, 1 - c, c)
            block = hid[2 * (2 * chip + core) + k % 2].reshape(tok, depth)
            parts[k, j] = lax.dot_general(
                head_ref[...], block, (((1,), (1,)), ((), ())), preferred_element_type=F32
            )
            return carry

        lax.fori_loop(0, 2, one, 0)
        swap(k).start()

    def send_cross(k):
        swap(k).wait()
        cross_out[k] = parts[k, 1] + swap_in[k]
        cross(k).start()

    forward(0)
    load_head.wait()
    arrive(0)
    partial_sums(0)
    send_cross(0)
    if n_zh >= 4:
        hear(0)
        tell(1)
    forward(1)
    arrive(1)
    partial_sums(1)
    send_cross(1)
    if n_zh >= 4:
        hear(1)
        tell(2)
    partial_sums(2)
    partial_sums(3)
    load_teacher.wait()

    for h in range(2):
        cols = slice(h * tok, (h + 1) * tok)
        swap(2 + h).wait()
        stud[h] = parts[2 + h, 1] + swap_in[2 + h]
        cross(h).wait()
        s = stud[h] + cross_in[h]
        stud[h] = s
        t = teacher_ref[:, cols].astype(F32)
        top_s = jnp.max(s, axis=0, keepdims=True)
        top_t = jnp.max(t, axis=0, keepdims=True)
        exp_t = jnp.exp(t - top_t)
        stats = (
            top_s,
            jnp.sum(jnp.exp(s - top_s), axis=0, keepdims=True),
            top_t,
            jnp.sum(exp_t, axis=0, keepdims=True),
            jnp.sum(exp_t * (t - s), axis=0, keepdims=True),
        )
        for row, value in enumerate(stats):
            st_dp[d, row : row + 1, cols] = value

    to_partner(d).wait_send()
    for i in range(2):
        for peer in column.others():
            to_column(2 * y + i, peer).wait_send()
    for block in [partner] + blocks_of(0) + blocks_of(1):
        for side in range(2):
            to_ring(block, side, z % 2).wait_send()

    def share(group, held, send, recv):
        gather_start(group, held.at[group.me], held, send, recv)
        gather_wait(group, held.at[group.me], held, send, recv)
        return merge(held, group.n)

    store_stats(st_zl.at[mine], share(dp, st_dp, sdp_s, sdp_r))
    store_stats(st_zh.at[zh], share(near, st_zl, szl_s, szl_r))
    if n_zh >= 4:
        hear(2)
    top_s, sum_s, top_t, sum_t, cross_term = share(far, st_zh, szh_s, szh_r)
    position = lax.broadcasted_iota(jnp.int32, (1, 2 * tok), 1)
    mask = jnp.where(position >= start_ref[m], 1.0, 0.0).astype(F32)
    scale_s, scale_t = mask / sum_s, mask / sum_t

    def grad_x(h):
        block = grads.at[2 * m + h]
        return mp.copy(block, block, gx_s.at[h], gx_r.at[h], other_chip)

    def grad_c(h):
        block = grads.at[2 * m + h]
        return mp.copy(block, block, gc_s.at[h], gc_r.at[h], other_core)

    def grad_d(h):
        block = grads.at[2 * other_chip + h]
        return mp.copy(block, block, gd_s.at[h], gd_r.at[h], other_core)

    for h in range(2):
        cols = slice(h * tok, (h + 1) * tok)
        exp_s = jnp.exp(stud[h] - top_s[:, cols])
        exp_t = jnp.exp(teacher_ref[:, cols].astype(F32) - top_t[:, cols])
        grads[2 * m + h] = (exp_s * scale_s[:, cols] - exp_t * scale_t[:, cols]).astype(BF16)
        grad_x(h).start()
        grad_c(h).start()
    kl_ref[...] = mask * (cross_term / sum_t - top_t - jnp.log(sum_t) + top_s + jnp.log(sum_s))

    def to_neighbour(block, side):
        return ring.copy(
            gh_out.at[block, 2 * (1 - parity) + side],
            gz_in.at[block, side],
            gz_s.at[block, side],
            gz_r.at[block, side],
            (up, down)[side],
        )

    def owner_copy(block):
        return dp.copy(gh_mid.at[block], gh_in.at[d], gh_s.at[block], gh_r.at[d], block)

    def hidden_terms(block):
        gh_out[block] = (
            lax.dot_general(
                grads[block], head_ref[...], (((0,), (0,)), ((), ())), preferred_element_type=F32
            )
            .astype(BF16)
            .reshape(4, sub, depth)
        )
        for side in range(2):
            to_neighbour(block, side).start()

    def hand_over(block):
        for side in range(2):
            to_neighbour(block, side).wait()
            own_rows = gh_out[block, 2 * parity + side].astype(F32)
            gh_mid[block, side] = (own_rows + gz_in[block, side].astype(F32)).astype(BF16)

        @pl.when(block != d)
        def _():
            owner_copy(block).start()

    for h in range(2):
        hidden_terms(2 * m + h)
    for h in range(2):
        grad_c(h).wait()
        hidden_terms(2 * other_core + h)
    for h in range(2):
        hand_over(2 * m + h)
    for h in range(2):
        grad_x(h).wait()
        grad_d(h).start()
        hidden_terms(2 * other_chip + h)
        hand_over(2 * other_core + h)
    for h in range(2):
        grad_d(h).wait()
        hidden_terms(2 * diagonal + h)
    for h in range(2):
        hand_over(2 * other_chip + h)
    for h in range(2):
        hand_over(2 * diagonal + h)

    scatter_wait(dp, gh_mid, gh_in, gh_s, gh_r)
    gh_in[d] = gh_mid[d]
    few = tok // n_z
    each = sub // few
    for side in range(2):
        total = gh_in[0, side].astype(F32)
        for i in range(1, n_dp):
            total = total + gh_in[i, side].astype(F32)
        for i in range(each):
            zs_out[side * each + i] = total[i * few : (i + 1) * few, :].astype(BF16)
    scatter_start(alike, zs_out, zs_in, zs_s, zs_r)

    def head_step(block, carry):
        tokens = hid[block].reshape(tok, depth)
        head_acc[...] += jnp.dot(grads[block], tokens, preferred_element_type=F32)
        return carry

    head_acc[...] = jnp.zeros_like(head_acc)
    lax.fori_loop(0, n_dp, head_step, 0)
    head_out[...] = head_acc[...].astype(BF16)
    store_head = pltpu.make_async_copy(head_out, grad_head_hbm, local_sem.at[3])
    store_head.start()

    scatter_wait(alike, zs_out, zs_in, zs_s, zs_r)
    me = alike.me
    zs_in[me] = zs_out[me]
    total = zs_in[0].astype(F32)
    for i in range(1, alike.n):
        total = total + zs_in[i].astype(F32)
    fin[me] = total.astype(BF16)
    gather_start(alike, fin.at[me], fin, fa_s, fa_r)
    gather_wait(alike, fin.at[me], fin, fa_s, fa_r)

    def exchange(side):
        return ring.copy(
            fin.at[pl.ds(side * each, each)],
            fin_other.at[side],
            fo_s.at[side],
            fo_r.at[side],
            (up, down)[side],
        )

    for side in range(2):
        exchange(side).start()
    for side in range(2):
        for i in range(each):
            rows = slice(i * few, (i + 1) * few)
            grad_hidden_ref[2 * parity + side, rows, :] = fin[side * each + i].astype(F32)
    for side in range(2):
        exchange(side).wait()
        for i in range(each):
            rows = slice(i * few, (i + 1) * few)
            grad_hidden_ref[2 * (1 - parity) + side, rows, :] = fin_other[side, i].astype(F32)
    store_head.wait()


def copy_kernel(*refs):
    sources, results, held, (load, store) = refs[:3], refs[3:6], refs[6:9], refs[9:]
    loads = [pltpu.make_async_copy(a, b, load.at[i]) for i, (a, b) in enumerate(zip(sources, held))]
    stores = [pltpu.make_async_copy(a, b, store.at[i]) for i, (a, b) in enumerate(zip(held, results))]
    for copy in loads:
        copy.start()
    for before, after in zip(loads, stores):
        before.wait()
        after.start()
    for copy in stores:
        copy.wait()


def solution(mesh):
    n_dp, n_z, n_mp = mesh.shape["dp"], mesh.shape["vocab"], mesh.shape["mp"]
    n_zl = min(4, n_z)
    n_zh = n_z // n_zl

    def per_device(hidden, head_weight, teacher_logits, response_start):
        tok, depth = hidden.shape
        own, cols = teacher_logits.shape
        assert n_mp == 4 and own == 2 * tok == LEN and n_dp == 8 and n_zl == 4 and n_zh == 8
        few = tok // n_z
        dma = pltpu.SemaphoreType.DMA
        vmem = pl.BlockSpec(memory_space=pltpu.VMEM)
        hbm = pl.BlockSpec(memory_space=pl.ANY)
        shapes = (
            jax.ShapeDtypeStruct((1, own), F32),
            jax.ShapeDtypeStruct((4, tok // 4, depth), F32),
            jax.ShapeDtypeStruct((cols, depth), BF16),
        )
        results = pl.pallas_call(
            functools.partial(kernel, (n_dp, n_z, n_zl, n_zh)),
            name="distill",
            out_shape=shapes,
            in_specs=[hbm, hbm, hbm, pl.BlockSpec(memory_space=pltpu.SMEM)],
            out_specs=(vmem, vmem, hbm),
            scratch_shapes=[
                pltpu.VMEM((cols, depth), BF16),
                pltpu.VMEM((cols, own), BF16),
                pltpu.VMEM((cols, depth), BF16),
                pltpu.VMEM((n_dp, 4, tok // 4, depth), BF16),
                pltpu.VMEM((4, 2, cols, tok), F32),
                pltpu.VMEM((4, cols, tok), F32),
                pltpu.VMEM((2, cols, tok), F32),
                pltpu.VMEM((2, cols, tok), F32),
                pltpu.VMEM((2, cols, tok), F32),
                pltpu.VMEM((n_dp, 8, own), F32),
                pltpu.VMEM((n_zl, 8, own), F32),
                pltpu.VMEM((n_zh, 8, own), F32),
                pltpu.VMEM((n_dp, cols, tok), BF16),
                pltpu.VMEM((n_dp, 4, tok // 4, depth), BF16),
                pltpu.VMEM((n_dp, 2, tok // 4, depth), BF16),
                pltpu.VMEM((n_dp, 2, tok // 4, depth), BF16),
                pltpu.VMEM((n_dp, 2, tok // 4, depth), BF16),
                pltpu.VMEM((n_z // 2, few, depth), BF16),
                pltpu.VMEM((n_z // 2, few, depth), BF16),
                pltpu.VMEM((n_z // 2, few, depth), BF16),
                pltpu.VMEM((2, n_z // 4, few, depth), BF16),
                pltpu.VMEM((cols, depth), F32),
                dma((4,)),
                pltpu.SemaphoreType.REGULAR((3,)),
                dma, dma,
                dma((2, n_dp // 2)), dma((n_dp,)),
                dma((n_dp, 2)), dma((n_dp, 2)),
                dma((4,)), dma((4,)),
                dma((2,)), dma((2,)),
                dma((n_dp,)), dma((n_dp,)),
                dma((n_zl,)), dma((n_zl,)),
                dma((n_zh,)), dma((n_zh,)),
                dma((2,)), dma((2,)),
                dma((2,)), dma((2,)),
                dma((2,)), dma((2,)),
                dma((n_dp, 2)), dma((n_dp, 2)),
                dma((n_dp,)), dma((n_dp,)),
                dma((n_z // 2,)), dma((n_z // 2,)),
                dma((n_z // 2,)), dma((n_z // 2,)),
                dma((2,)), dma((2,)),
            ],
            compiler_params=pltpu.CompilerParams(
                collective_id=0, has_side_effects=True, vmem_limit_bytes=56 << 20
            ),
        )(hidden.reshape(4, tok // 4, depth), head_weight.T, teacher_logits.T, response_start)
        kl, grad_hidden, grad_head = pl.pallas_call(
            copy_kernel,
            name="results",
            out_shape=shapes,
            in_specs=[hbm, hbm, hbm],
            out_specs=(hbm, hbm, hbm),
            scratch_shapes=[pltpu.VMEM(s.shape, s.dtype) for s in shapes] + [dma((3,)), dma((3,))],
        )(*results)
        return kl.reshape(own), grad_hidden.reshape(tok, depth), grad_head.T

    return jax.shard_map(
        per_device,
        mesh=mesh,
        in_specs=(P("dp", "mp"), P("mp", ("dp", "vocab")), P("mp", ("dp", "vocab")), P()),
        out_specs=(P("mp"), P("dp", "mp"), P("mp", ("dp", "vocab"))),
        check_vma=False,
    )
```

```python
import functools

import jax
import jax.numpy as jnp
from jax import lax
from jax.experimental import pallas as pl
from jax.experimental.pallas import tpu as pltpu
from jax.sharding import PartitionSpec as P

LEN = 256
MESH = pl.DeviceIdType.MESH
F32 = jnp.float32
BF16 = jnp.bfloat16

ROW_MS, ROW_SS, ROW_MT, ROW_ST, ROW_C = range(5)


class Group:
    def __init__(self, n, me, device):
        self.n, self.me, self.device = n, me, device

    def others(self):
        shifts = sorted(range(1, self.n), key=lambda k: -min(k, self.n - k))
        return [lax.rem(self.me + k, self.n) for k in shifts]

    def copy(self, src, dst, send, recv, to):
        return pltpu.make_async_remote_copy(
            src_ref=src,
            dst_ref=dst,
            send_sem=send,
            recv_sem=recv,
            device_id=self.device(to),
            device_id_type=MESH,
        )


def gather_start(group, src, held, send, recv):
    for peer in group.others():
        group.copy(src, held.at[group.me], send.at[peer], recv.at[group.me], peer).start()


def gather_wait(group, src, held, send, recv):
    for peer in group.others():
        copy = group.copy(src, held.at[peer], send.at[peer], recv.at[peer], peer)
        copy.wait_recv()
        copy.wait_send()


def scatter_start(group, parts, held, send, recv):
    for peer in group.others():
        group.copy(parts.at[peer], held.at[group.me], send.at[peer], recv.at[group.me], peer).start()


def scatter_wait(group, parts, held, send, recv):
    for peer in group.others():
        copy = group.copy(parts.at[peer], held.at[peer], send.at[peer], recv.at[peer], peer)
        copy.wait_recv()
        copy.wait_send()


def merge(held, n):
    rows = [[held[i, r : r + 1, :] for r in range(5)] for i in range(n)]
    top_s = functools.reduce(jnp.maximum, [row[ROW_MS] for row in rows])
    top_t = functools.reduce(jnp.maximum, [row[ROW_MT] for row in rows])
    sum_s = sum_t = cross = None
    for row in rows:
        scale_s = jnp.exp(row[ROW_MS] - top_s)
        scale_t = jnp.exp(row[ROW_MT] - top_t)
        terms = row[ROW_SS] * scale_s, row[ROW_ST] * scale_t, row[ROW_C] * scale_t
        if sum_s is None:
            sum_s, sum_t, cross = terms
        else:
            sum_s, sum_t, cross = sum_s + terms[0], sum_t + terms[1], cross + terms[2]
    return top_s, sum_s, top_t, sum_t, cross


def store_stats(ref, stats):
    for row, value in enumerate(stats):
        ref[row : row + 1, :] = value


def kernel(
    sizes,
    hidden_ref, head_hbm, teacher_hbm, start_ref,
    kl_ref, grad_hidden_ref, grad_head_hbm,
    head_ref, teacher_ref, head_out, student_exp, scales,
    hid, parts, swap_in, cross_out, cross_in,
    st_dp, st_zl, st_zh, grads, gh_out, gz_in, gh_mid, gh_in,
    zs_out, zs_in, fin, fin_other, head_acc,
    local_sem, teacher_sem, ready, hx_s, hx_r, hy_s, hy_r, hz_s, hz_r,
    swap_s, swap_r, cross_s, cross_r,
    sdp_s, sdp_r, szl_s, szl_r, szh_s, szh_r,
    t_s, t_r, e_s, e_r, sc_s, sc_r, gz_s, gz_r, gh_s, gh_r,
    zs_s, zs_r, fa_s, fa_r, fo_s, fo_r,
):
    n_dp, n_z, n_zl, n_zh = sizes
    n_y = n_dp // 2
    sub, depth = hidden_ref.shape[1:]
    tok = 4 * sub
    d, z, m = lax.axis_index("dp"), lax.axis_index("vocab"), lax.axis_index("mp")
    x, c = m // 2, m % 2
    y = d // 2
    partner = 2 * y + (1 - d % 2)
    zl, zh = z % n_zl, z // n_zl
    other_core, other_chip = 2 * x + (1 - c), 2 * (1 - x) + c
    diagonal = 2 * (1 - x) + (1 - c)
    parity = z % 2
    up, down = lax.rem(z + 1, n_z), lax.rem(z + n_z - 1, n_z)

    dp = Group(n_dp, d, lambda i: (i, z, m))
    column = Group(n_y, y, lambda i: (2 * i + d % 2, z, m))
    ring = Group(n_z, z, lambda i: (d, i, m))
    mine = 2 * (zl % 2) + zl // 2
    near = Group(n_zl, mine, lambda i: (d, zh * n_zl + 2 * (i % 2) + i // 2, m))
    alike = Group(n_z // 2, z // 2, lambda i: (d, 2 * i + parity, m))
    far = Group(n_zh, zh, lambda i: (d, i * n_zl + zl, m))
    mp = Group(4, m, lambda i: (d, z, i))
    far_next = [far.device(lax.rem(zh + k, n_zh)) for k in (1, n_zh - 1)]

    barrier = pltpu.get_barrier_semaphore()
    peers = [g.device(p) for g in (dp, near) for p in g.others()] + far_next
    peers += [mp.device(p) for p in mp.others()] + [ring.device(up), ring.device(down)]
    peers += [ring.device(lax.rem(z + k, n_z)) for k in (2, n_z - 2)]
    for peer in peers:
        pl.semaphore_signal(barrier, inc=1, device_id=peer, device_id_type=MESH)
    own = pltpu.make_async_copy(hidden_ref, hid.at[d], local_sem.at[0])
    own.start()
    load_head = pltpu.make_async_copy(head_hbm, head_ref, local_sem.at[1])
    load_head.start()
    load_teacher = [
        pltpu.make_async_copy(
            teacher_hbm.at[:, pl.ds(h * tok, tok)], teacher_ref.at[2 * m + h], teacher_sem.at[h]
        )
        for h in range(2)
    ]
    for load in load_teacher:
        load.start()
    own.wait()
    pl.semaphore_wait(barrier, len(peers))

    def tell(r):
        for peer in far_next:
            pl.semaphore_signal(ready.at[r], inc=1, device_id=peer, device_id_type=MESH)

    def hear(r):
        pl.semaphore_wait(ready.at[r], 2)

    half = pl.ds(2 * (z % 2), 2)

    def to_partner(block):
        part = hid.at[block, half]
        return dp.copy(part, part, hx_s, hx_r, partner)

    def to_column(block, peer):
        part = hid.at[block, half]
        return column.copy(part, part, hy_s.at[block % 2, peer], hy_r.at[block], peer)

    def to_ring(block, side, parity):
        part = hid.at[block, 2 * parity + side]
        return ring.copy(part, part, hz_s.at[block, side], hz_r.at[block, side], (up, down)[side])

    def pass_on(block):
        for side in range(2):
            to_ring(block, side, z % 2).start()

    class Spread:
        def __init__(self, held, send, recv):
            self.held, self.send, self.recv = held, send, recv

        def hop(self, way, block, h, to):
            part = self.held.at[block]
            return mp.copy(part, part, self.send.at[way, h], self.recv.at[way, h], to)

        def chip(self, h):
            return self.hop(0, 2 * m + h, h, other_chip)

        def core(self, h):
            return self.hop(1, 2 * m + h, h, other_core)

        def onward(self, h):
            return self.hop(2, 2 * other_chip + h, h, other_core)

        def start(self):
            for h in range(2):
                self.chip(h).start()
                self.core(h).start()

        def turn(self, h):
            self.chip(h).wait()
            self.onward(h).start()

        def finish(self):
            for h in range(2):
                self.core(h).wait()
                self.onward(h).wait()

    teacher = Spread(teacher_ref, t_s, t_r)
    student = Spread(student_exp, e_s, e_r)

    to_partner(d).start()
    for i in range(2):
        block = 2 * y + i

        @pl.when(block != d)
        def _():
            to_partner(partner).wait_recv()

        for peer in column.others():
            to_column(block, peer).start()
    pass_on(partner)
    if n_zh >= 4:
        tell(0)
    for load in load_teacher:
        load.wait()
    teacher.start()

    def blocks_of(i):
        return [2 * row + i for row in reversed(column.others())]

    def forward(i):
        for block in blocks_of(i):
            to_column(block, block // 2).wait_recv()
            pass_on(block)

    def arrive(i):
        for block in blocks_of(i):
            for side in range(2):
                to_ring(block, side, 1 - z % 2).wait_recv()

        @pl.when(2 * y + i != d)
        def _():
            for side in range(2):
                to_ring(partner, side, 1 - z % 2).wait_recv()

    def swap(k):
        return mp.copy(parts.at[k, 0], swap_in.at[k], swap_s.at[k], swap_r.at[k], other_core)

    def cross(k):
        return mp.copy(cross_out.at[k], cross_in.at[k], cross_s.at[k], cross_r.at[k], other_chip)

    def partial_sums(k):
        chip = (1 - x) if k < 2 else x

        def one(j, carry):
            core = jnp.where(j == 0, 1 - c, c)
            block = hid[2 * (2 * chip + core) + k % 2].reshape(tok, depth)
            parts[k, j] = lax.dot_general(
                head_ref[...], block, (((1,), (1,)), ((), ())), preferred_element_type=F32
            )
            return carry

        lax.fori_loop(0, 2, one, 0)
        swap(k).start()

    def send_cross(k):
        swap(k).wait()
        cross_out[k] = parts[k, 1] + swap_in[k]
        cross(k).start()

    forward(0)
    load_head.wait()
    arrive(0)
    partial_sums(0)
    send_cross(0)
    if n_zh >= 4:
        hear(0)
        tell(1)
    forward(1)
    arrive(1)
    partial_sums(1)
    send_cross(1)
    if n_zh >= 4:
        hear(1)
        tell(2)
    partial_sums(2)
    partial_sums(3)
    for h in range(2):
        teacher.turn(h)

    for h in range(2):
        cols = slice(h * tok, (h + 1) * tok)
        swap(2 + h).wait()
        cross(h).wait()
        s = parts[2 + h, 1] + swap_in[2 + h] + cross_in[h]
        t = teacher_ref[2 * m + h].astype(F32)
        top_s = jnp.max(s, axis=0, keepdims=True)
        top_t = jnp.max(t, axis=0, keepdims=True)
        exp_s = jnp.exp(s - top_s)
        exp_t = jnp.exp(t - top_t)
        student_exp[2 * m + h] = exp_s.astype(BF16)
        stats = (
            top_s,
            jnp.sum(exp_s, axis=0, keepdims=True),
            top_t,
            jnp.sum(exp_t, axis=0, keepdims=True),
            jnp.sum(exp_t * (t - s), axis=0, keepdims=True),
        )
        for row, value in enumerate(stats):
            st_dp[d, row : row + 1, cols] = value

    to_partner(d).wait_send()
    for i in range(2):
        for peer in column.others():
            to_column(2 * y + i, peer).wait_send()
    for block in [partner] + blocks_of(0) + blocks_of(1):
        for side in range(2):
            to_ring(block, side, z % 2).wait_send()

    def share(group, held, send, recv, between=None):
        gather_start(group, held.at[group.me], held, send, recv)
        if between is not None:
            between()
        gather_wait(group, held.at[group.me], held, send, recv)
        return merge(held, group.n)

    def turns():
        for h in range(2):
            student.turn(h)
        teacher.finish()

    own_top_s = st_dp[d, ROW_MS : ROW_MS + 1, :]
    store_stats(st_zl.at[mine], share(dp, st_dp, sdp_s, sdp_r))
    student.start()
    store_stats(st_zh.at[zh], share(near, st_zl, szl_s, szl_r))
    if n_zh >= 4:
        hear(2)
    top_s, sum_s, top_t, sum_t, cross_term = share(far, st_zh, szh_s, szh_r, turns)
    position = lax.broadcasted_iota(jnp.int32, (1, 2 * tok), 1)
    mask = jnp.where(position >= start_ref[m], 1.0, 0.0).astype(F32)
    scales[m, 0:1, :] = mask * jnp.exp(own_top_s - top_s) / sum_s
    scales[m, 1:2, :] = mask / sum_t
    scales[m, 2:3, :] = top_t
    gather_start(mp, scales.at[m], scales, sc_s, sc_r)
    kl_ref[...] = mask * (cross_term / sum_t - top_t - jnp.log(sum_t) + top_s + jnp.log(sum_s))

    def logit_grads(quarter, h):
        cols = slice(h * tok, (h + 1) * tok)
        block = 2 * quarter + h
        exp_t = jnp.exp(teacher_ref[block].astype(F32) - scales[quarter, 2:3, cols])
        grads[block] = (
            student_exp[block].astype(F32) * scales[quarter, 0:1, cols] - exp_t * scales[quarter, 1:2, cols]
        ).astype(BF16)

    def to_neighbour(block, side):
        return ring.copy(
            gh_out.at[block, 2 * (1 - parity) + side],
            gz_in.at[block, side],
            gz_s.at[block, side],
            gz_r.at[block, side],
            (up, down)[side],
        )

    def owner_copy(block):
        return dp.copy(gh_mid.at[block], gh_in.at[d], gh_s.at[block], gh_r.at[d], block)

    def hidden_terms(quarter, h):
        logit_grads(quarter, h)
        block = 2 * quarter + h
        gh_out[block] = (
            lax.dot_general(
                grads[block], head_ref[...], (((0,), (0,)), ((), ())), preferred_element_type=F32
            )
            .astype(BF16)
            .reshape(4, sub, depth)
        )
        for side in range(2):
            to_neighbour(block, side).start()

    def hand_over(block):
        for side in range(2):
            to_neighbour(block, side).wait()
            own_rows = gh_out[block, 2 * parity + side].astype(F32)
            gh_mid[block, side] = (own_rows + gz_in[block, side].astype(F32)).astype(BF16)

        @pl.when(block != d)
        def _():
            owner_copy(block).start()

    for h in range(2):
        hidden_terms(m, h)
    student.finish()
    gather_wait(mp, scales.at[m], scales, sc_s, sc_r)
    order = (m, other_core, other_chip, diagonal)
    for i in range(1, 4):
        for h in range(2):
            hidden_terms(order[i], h)
            hand_over(2 * order[i - 1] + h)
    for h in range(2):
        hand_over(2 * diagonal + h)

    scatter_wait(dp, gh_mid, gh_in, gh_s, gh_r)
    gh_in[d] = gh_mid[d]
    few = tok // n_z
    each = sub // few
    for side in range(2):
        total = gh_in[0, side].astype(F32)
        for i in range(1, n_dp):
            total = total + gh_in[i, side].astype(F32)
        for i in range(each):
            zs_out[side * each + i] = total[i * few : (i + 1) * few, :].astype(BF16)
    scatter_start(alike, zs_out, zs_in, zs_s, zs_r)

    def head_step(block, carry):
        tokens = hid[block].reshape(tok, depth)
        head_acc[...] += jnp.dot(grads[block], tokens, preferred_element_type=F32)
        return carry

    head_acc[...] = jnp.zeros_like(head_acc)
    lax.fori_loop(0, n_dp, head_step, 0)
    head_out[...] = head_acc[...].astype(BF16)
    store_head = pltpu.make_async_copy(head_out, grad_head_hbm, local_sem.at[3])
    store_head.start()

    scatter_wait(alike, zs_out, zs_in, zs_s, zs_r)
    me = alike.me
    zs_in[me] = zs_out[me]
    total = zs_in[0].astype(F32)
    for i in range(1, alike.n):
        total = total + zs_in[i].astype(F32)
    fin[me] = total.astype(BF16)
    gather_start(alike, fin.at[me], fin, fa_s, fa_r)
    gather_wait(alike, fin.at[me], fin, fa_s, fa_r)

    def exchange(side):
        return ring.copy(
            fin.at[pl.ds(side * each, each)],
            fin_other.at[side],
            fo_s.at[side],
            fo_r.at[side],
            (up, down)[side],
        )

    for side in range(2):
        exchange(side).start()
    for side in range(2):
        for i in range(each):
            rows = slice(i * few, (i + 1) * few)
            grad_hidden_ref[2 * parity + side, rows, :] = fin[side * each + i].astype(F32)
    for side in range(2):
        exchange(side).wait()
        for i in range(each):
            rows = slice(i * few, (i + 1) * few)
            grad_hidden_ref[2 * (1 - parity) + side, rows, :] = fin_other[side, i].astype(F32)
    store_head.wait()


def copy_kernel(*refs):
    sources, results, held, (load, store) = refs[:3], refs[3:6], refs[6:9], refs[9:]
    loads = [pltpu.make_async_copy(a, b, load.at[i]) for i, (a, b) in enumerate(zip(sources, held))]
    stores = [pltpu.make_async_copy(a, b, store.at[i]) for i, (a, b) in enumerate(zip(held, results))]
    for copy in loads:
        copy.start()
    for before, after in zip(loads, stores):
        before.wait()
        after.start()
    for copy in stores:
        copy.wait()


def solution(mesh):
    n_dp, n_z, n_mp = mesh.shape["dp"], mesh.shape["vocab"], mesh.shape["mp"]
    n_zl = min(4, n_z)
    n_zh = n_z // n_zl

    def per_device(hidden, head_weight, teacher_logits, response_start):
        tok, depth = hidden.shape
        own, cols = teacher_logits.shape
        assert n_mp == 4 and own == 2 * tok == LEN and n_dp == 8 and n_zl == 4 and n_zh == 8
        few = tok // n_z
        dma = pltpu.SemaphoreType.DMA
        vmem = pl.BlockSpec(memory_space=pltpu.VMEM)
        hbm = pl.BlockSpec(memory_space=pl.ANY)
        shapes = (
            jax.ShapeDtypeStruct((1, own), F32),
            jax.ShapeDtypeStruct((4, tok // 4, depth), F32),
            jax.ShapeDtypeStruct((cols, depth), BF16),
        )
        results = pl.pallas_call(
            functools.partial(kernel, (n_dp, n_z, n_zl, n_zh)),
            name="distill",
            out_shape=shapes,
            in_specs=[hbm, hbm, hbm, pl.BlockSpec(memory_space=pltpu.SMEM)],
            out_specs=(vmem, vmem, hbm),
            scratch_shapes=[
                pltpu.VMEM((cols, depth), BF16),
                pltpu.VMEM((n_dp, cols, tok), BF16),
                pltpu.VMEM((cols, depth), BF16),
                pltpu.VMEM((n_dp, cols, tok), BF16),
                pltpu.VMEM((4, 8, own), F32),
                pltpu.VMEM((n_dp, 4, tok // 4, depth), BF16),
                pltpu.VMEM((4, 2, cols, tok), F32),
                pltpu.VMEM((4, cols, tok), F32),
                pltpu.VMEM((2, cols, tok), F32),
                pltpu.VMEM((2, cols, tok), F32),
                pltpu.VMEM((n_dp, 8, own), F32),
                pltpu.VMEM((n_zl, 8, own), F32),
                pltpu.VMEM((n_zh, 8, own), F32),
                pltpu.VMEM((n_dp, cols, tok), BF16),
                pltpu.VMEM((n_dp, 4, tok // 4, depth), BF16),
                pltpu.VMEM((n_dp, 2, tok // 4, depth), BF16),
                pltpu.VMEM((n_dp, 2, tok // 4, depth), BF16),
                pltpu.VMEM((n_dp, 2, tok // 4, depth), BF16),
                pltpu.VMEM((n_z // 2, few, depth), BF16),
                pltpu.VMEM((n_z // 2, few, depth), BF16),
                pltpu.VMEM((n_z // 2, few, depth), BF16),
                pltpu.VMEM((2, n_z // 4, few, depth), BF16),
                pltpu.VMEM((cols, depth), F32),
                dma((4,)),
                dma((2,)),
                pltpu.SemaphoreType.REGULAR((3,)),
                dma, dma,
                dma((2, n_dp // 2)), dma((n_dp,)),
                dma((n_dp, 2)), dma((n_dp, 2)),
                dma((4,)), dma((4,)),
                dma((2,)), dma((2,)),
                dma((n_dp,)), dma((n_dp,)),
                dma((n_zl,)), dma((n_zl,)),
                dma((n_zh,)), dma((n_zh,)),
                dma((3, 2)), dma((3, 2)),
                dma((3, 2)), dma((3, 2)),
                dma((4,)), dma((4,)),
                dma((n_dp, 2)), dma((n_dp, 2)),
                dma((n_dp,)), dma((n_dp,)),
                dma((n_z // 2,)), dma((n_z // 2,)),
                dma((n_z // 2,)), dma((n_z // 2,)),
                dma((2,)), dma((2,)),
            ],
            compiler_params=pltpu.CompilerParams(
                collective_id=0, has_side_effects=True, vmem_limit_bytes=56 << 20
            ),
        )(hidden.reshape(4, tok // 4, depth), head_weight.T, teacher_logits.T, response_start)
        kl, grad_hidden, grad_head = pl.pallas_call(
            copy_kernel,
            name="results",
            out_shape=shapes,
            in_specs=[hbm, hbm, hbm],
            out_specs=(hbm, hbm, hbm),
            scratch_shapes=[pltpu.VMEM(s.shape, s.dtype) for s in shapes] + [dma((3,)), dma((3,))],
        )(*results)
        return kl.reshape(own), grad_hidden.reshape(tok, depth), grad_head.T

    return jax.shard_map(
        per_device,
        mesh=mesh,
        in_specs=(P("dp", "mp"), P("mp", ("dp", "vocab")), P("mp", ("dp", "vocab")), P()),
        out_specs=(P("mp"), P("dp", "mp"), P("mp", ("dp", "vocab"))),
        check_vma=False,
    )
```

```python
import functools

import jax
import jax.numpy as jnp
from jax import lax
from jax.experimental import pallas as pl
from jax.experimental.pallas import tpu as pltpu
from jax.sharding import PartitionSpec as P

LEN = 256
MESH = pl.DeviceIdType.MESH
F32 = jnp.float32
BF16 = jnp.bfloat16

ROW_MS, ROW_SS, ROW_MT, ROW_ST, ROW_C = range(5)


class Group:
    def __init__(self, n, me, device):
        self.n, self.me, self.device = n, me, device

    def others(self):
        shifts = sorted(range(1, self.n), key=lambda k: -min(k, self.n - k))
        return [lax.rem(self.me + k, self.n) for k in shifts]

    def copy(self, src, dst, send, recv, to):
        return pltpu.make_async_remote_copy(
            src_ref=src,
            dst_ref=dst,
            send_sem=send,
            recv_sem=recv,
            device_id=self.device(to),
            device_id_type=MESH,
        )


def gather_start(group, src, held, send, recv):
    for peer in group.others():
        group.copy(src, held.at[group.me], send.at[peer], recv.at[group.me], peer).start()


def gather_wait(group, src, held, send, recv):
    for peer in group.others():
        copy = group.copy(src, held.at[peer], send.at[peer], recv.at[peer], peer)
        copy.wait_recv()
        copy.wait_send()


def scatter_start(group, parts, held, send, recv):
    for peer in group.others():
        group.copy(parts.at[peer], held.at[group.me], send.at[peer], recv.at[group.me], peer).start()


def scatter_wait(group, parts, held, send, recv):
    for peer in group.others():
        copy = group.copy(parts.at[peer], held.at[peer], send.at[peer], recv.at[peer], peer)
        copy.wait_recv()
        copy.wait_send()


def merge(held, n):
    rows = [[held[i, r : r + 1, :] for r in range(5)] for i in range(n)]
    top_s = functools.reduce(jnp.maximum, [row[ROW_MS] for row in rows])
    top_t = functools.reduce(jnp.maximum, [row[ROW_MT] for row in rows])
    sum_s = sum_t = cross = None
    for row in rows:
        scale_s = jnp.exp(row[ROW_MS] - top_s)
        scale_t = jnp.exp(row[ROW_MT] - top_t)
        terms = row[ROW_SS] * scale_s, row[ROW_ST] * scale_t, row[ROW_C] * scale_t
        if sum_s is None:
            sum_s, sum_t, cross = terms
        else:
            sum_s, sum_t, cross = sum_s + terms[0], sum_t + terms[1], cross + terms[2]
    return top_s, sum_s, top_t, sum_t, cross


def store_stats(ref, stats):
    for row, value in enumerate(stats):
        ref[row : row + 1, :] = value


def kernel(
    sizes,
    hidden_ref, head_hbm, teacher_hbm, start_ref,
    kl_ref, grad_hidden_ref, grad_head_hbm,
    head_ref, teacher_ref, head_out, student_exp, scales,
    hid, parts, swap_in, cross_out, cross_in,
    st_dp, st_zl, st_zh, grads, gh_out, gz_in, gh_mid, gh_in,
    zs_out, zs_in, fin, fin_other, head_acc,
    local_sem, teacher_sem, ready, hx_s, hx_r, hy_s, hy_r, hz_s, hz_r,
    swap_s, swap_r, cross_s, cross_r,
    sdp_s, sdp_r, szl_s, szl_r, szh_s, szh_r,
    t_s, t_r, e_s, e_r, sc_s, sc_r, gz_s, gz_r, gh_s, gh_r,
    zs_s, zs_r, fa_s, fa_r, fo_s, fo_r,
):
    n_dp, n_z, n_zl, n_zh = sizes
    n_y = n_dp // 2
    sub, depth = hidden_ref.shape[1:]
    tok = 4 * sub
    d, z, m = lax.axis_index("dp"), lax.axis_index("vocab"), lax.axis_index("mp")
    x, c = m // 2, m % 2
    y = d // 2
    partner = 2 * y + (1 - d % 2)
    zl, zh = z % n_zl, z // n_zl
    other_core, other_chip = 2 * x + (1 - c), 2 * (1 - x) + c
    diagonal = 2 * (1 - x) + (1 - c)
    parity = z % 2
    up, down = lax.rem(z + 1, n_z), lax.rem(z + n_z - 1, n_z)

    dp = Group(n_dp, d, lambda i: (i, z, m))
    column = Group(n_y, y, lambda i: (2 * i + d % 2, z, m))
    ring = Group(n_z, z, lambda i: (d, i, m))
    mine = 2 * (zl % 2) + zl // 2
    near = Group(n_zl, mine, lambda i: (d, zh * n_zl + 2 * (i % 2) + i // 2, m))
    alike = Group(n_z // 2, z // 2, lambda i: (d, 2 * i + parity, m))
    far = Group(n_zh, zh, lambda i: (d, i * n_zl + zl, m))
    mp = Group(4, m, lambda i: (d, z, i))
    far_next = [far.device(lax.rem(zh + k, n_zh)) for k in (1, n_zh - 1)]

    barrier = pltpu.get_barrier_semaphore()
    peers = [g.device(p) for g in (dp, near) for p in g.others()] + far_next
    peers += [mp.device(p) for p in mp.others()] + [ring.device(up), ring.device(down)]
    peers += [ring.device(lax.rem(z + k, n_z)) for k in (2, n_z - 2)]
    for peer in peers:
        pl.semaphore_signal(barrier, inc=1, device_id=peer, device_id_type=MESH)
    own = pltpu.make_async_copy(hidden_ref, hid.at[d], local_sem.at[0])
    own.start()
    load_head = pltpu.make_async_copy(head_hbm, head_ref, local_sem.at[1])
    load_head.start()
    load_teacher = [
        pltpu.make_async_copy(
            teacher_hbm.at[:, pl.ds(h * tok, tok)], teacher_ref.at[2 * m + h], teacher_sem.at[h]
        )
        for h in range(2)
    ]
    for load in load_teacher:
        load.start()
    own.wait()
    pl.semaphore_wait(barrier, len(peers))

    def tell(r):
        for peer in far_next:
            pl.semaphore_signal(ready.at[r], inc=1, device_id=peer, device_id_type=MESH)

    def hear(r):
        pl.semaphore_wait(ready.at[r], 2)

    half = pl.ds(2 * (z % 2), 2)

    def to_partner(block):
        part = hid.at[block, half]
        return dp.copy(part, part, hx_s, hx_r, partner)

    def to_column(block, peer):
        part = hid.at[block, half]
        return column.copy(part, part, hy_s.at[block % 2, peer], hy_r.at[block], peer)

    def to_ring(block, side, parity):
        part = hid.at[block, 2 * parity + side]
        return ring.copy(part, part, hz_s.at[block, side], hz_r.at[block, side], (up, down)[side])

    def pass_on(block):
        for side in range(2):
            to_ring(block, side, z % 2).start()

    class Spread:
        def __init__(self, held, send, recv):
            self.held, self.send, self.recv = held, send, recv

        def hop(self, way, block, h, to):
            part = self.held.at[block]
            return mp.copy(part, part, self.send.at[way, h], self.recv.at[way, h], to)

        def chip(self, h):
            return self.hop(0, 2 * m + h, h, other_chip)

        def core(self, h):
            return self.hop(1, 2 * m + h, h, other_core)

        def onward(self, h):
            return self.hop(2, 2 * other_chip + h, h, other_core)

        def start(self):
            for h in range(2):
                self.chip(h).start()
                self.core(h).start()

        def turn(self, h):
            self.chip(h).wait()
            self.onward(h).start()

        def finish(self):
            for h in range(2):
                self.core(h).wait()
                self.onward(h).wait()

    teacher = Spread(teacher_ref, t_s, t_r)
    student = Spread(student_exp, e_s, e_r)

    to_partner(d).start()
    for i in range(2):
        block = 2 * y + i

        @pl.when(block != d)
        def _():
            to_partner(partner).wait_recv()

        for peer in column.others():
            to_column(block, peer).start()
    pass_on(partner)
    if n_zh >= 4:
        tell(0)
    for load in load_teacher:
        load.wait()
    teacher.start()

    def blocks_of(i):
        return [2 * row + i for row in reversed(column.others())]

    def forward(i):
        for block in blocks_of(i):
            to_column(block, block // 2).wait_recv()
            pass_on(block)

    def arrive(i):
        for block in blocks_of(i):
            for side in range(2):
                to_ring(block, side, 1 - z % 2).wait_recv()

        @pl.when(2 * y + i != d)
        def _():
            for side in range(2):
                to_ring(partner, side, 1 - z % 2).wait_recv()

    def swap(k):
        return mp.copy(parts.at[k, 0], swap_in.at[k], swap_s.at[k], swap_r.at[k], other_core)

    def cross(k):
        return mp.copy(cross_out.at[k], cross_in.at[k], cross_s.at[k], cross_r.at[k], other_chip)

    def partial_sums(k):
        chip = (1 - x) if k < 2 else x

        def one(j, carry):
            core = jnp.where(j == 0, 1 - c, c)
            block = hid[2 * (2 * chip + core) + k % 2].reshape(tok, depth)
            parts[k, j] = lax.dot_general(
                head_ref[...], block, (((1,), (1,)), ((), ())), preferred_element_type=F32
            )
            return carry

        lax.fori_loop(0, 2, one, 0)
        swap(k).start()

    def send_cross(k):
        swap(k).wait()
        cross_out[k] = parts[k, 1] + swap_in[k]
        cross(k).start()

    forward(0)
    load_head.wait()
    arrive(0)
    partial_sums(0)
    forward(1)
    send_cross(0)
    if n_zh >= 4:
        hear(0)
        tell(1)
    arrive(1)
    partial_sums(1)
    send_cross(1)
    if n_zh >= 4:
        hear(1)
        tell(2)
    partial_sums(2)
    partial_sums(3)
    for h in range(2):
        teacher.turn(h)

    for h in range(2):
        cols = slice(h * tok, (h + 1) * tok)
        swap(2 + h).wait()
        cross(h).wait()
        s = parts[2 + h, 1] + swap_in[2 + h] + cross_in[h]
        t = teacher_ref[2 * m + h].astype(F32)
        top_s = jnp.max(s, axis=0, keepdims=True)
        top_t = jnp.max(t, axis=0, keepdims=True)
        exp_s = jnp.exp(s - top_s)
        exp_t = jnp.exp(t - top_t)
        student_exp[2 * m + h] = exp_s.astype(BF16)
        stats = (
            top_s,
            jnp.sum(exp_s, axis=0, keepdims=True),
            top_t,
            jnp.sum(exp_t, axis=0, keepdims=True),
            jnp.sum(exp_t * (t - s), axis=0, keepdims=True),
        )
        for row, value in enumerate(stats):
            st_dp[d, row : row + 1, cols] = value

    to_partner(d).wait_send()
    for i in range(2):
        for peer in column.others():
            to_column(2 * y + i, peer).wait_send()
    for block in [partner] + blocks_of(0) + blocks_of(1):
        for side in range(2):
            to_ring(block, side, z % 2).wait_send()

    def share(group, held, send, recv, between=None):
        gather_start(group, held.at[group.me], held, send, recv)
        if between is not None:
            between()
        gather_wait(group, held.at[group.me], held, send, recv)
        return merge(held, group.n)

    def turns():
        for h in range(2):
            student.turn(h)
        teacher.finish()

    own_top_s = st_dp[d, ROW_MS : ROW_MS + 1, :]
    store_stats(st_zl.at[mine], share(dp, st_dp, sdp_s, sdp_r))
    student.start()
    store_stats(st_zh.at[zh], share(near, st_zl, szl_s, szl_r))
    if n_zh >= 4:
        hear(2)
    top_s, sum_s, top_t, sum_t, cross_term = share(far, st_zh, szh_s, szh_r, turns)
    position = lax.broadcasted_iota(jnp.int32, (1, 2 * tok), 1)
    mask = jnp.where(position >= start_ref[m], 1.0, 0.0).astype(F32)
    token_scales = mask * jnp.exp(own_top_s - top_s) / sum_s, mask / sum_t, top_t
    for h in range(2):
        for row, value in enumerate(token_scales):
            scales[m, h, row : row + 1, :] = value[:, h * tok : (h + 1) * tok]
    gather_start(mp, scales.at[m], scales, sc_s, sc_r)
    kl_ref[...] = mask * (cross_term / sum_t - top_t - jnp.log(sum_t) + top_s + jnp.log(sum_s))

    def logit_grads(block):
        scale_s, scale_t, top = [scales[block // 2, block % 2, row : row + 1, :] for row in range(3)]
        exp_t = jnp.exp(teacher_ref[block].astype(F32) - top)
        grads[block] = (student_exp[block].astype(F32) * scale_s - exp_t * scale_t).astype(BF16)

    def to_neighbour(block, side):
        return ring.copy(
            gh_out.at[block, 2 * (1 - parity) + side],
            gz_in.at[block, side],
            gz_s.at[block, side],
            gz_r.at[block, side],
            (up, down)[side],
        )

    def owner_copy(block):
        return dp.copy(gh_mid.at[block], gh_in.at[d], gh_s.at[block], gh_r.at[d], block)

    def hidden_terms(block):
        logit_grads(block)
        gh_out[block] = (
            lax.dot_general(
                grads[block], head_ref[...], (((0,), (0,)), ((), ())), preferred_element_type=F32
            )
            .astype(BF16)
            .reshape(4, sub, depth)
        )
        for side in range(2):
            to_neighbour(block, side).start()

    def hand_over(block):
        for side in range(2):
            to_neighbour(block, side).wait()
            own_rows = gh_out[block, 2 * parity + side].astype(F32)
            gh_mid[block, side] = (own_rows + gz_in[block, side].astype(F32)).astype(BF16)

        @pl.when(block != d)
        def _():
            owner_copy(block).start()

    student.finish()
    gather_wait(mp, scales.at[m], scales, sc_s, sc_r)
    shifts = ((2, 1), (2, 0), (1, 1), (3, 1), (1, 0), (3, 0), (0, 1), (0, 0))
    order = [2 * lax.rem(y + dy, n_y) + (d + dx) % 2 for dy, dx in shifts]
    hidden_terms(order[0])
    for before, block in zip(order[:-1], order[1:]):
        hidden_terms(block)
        hand_over(before)
    hand_over(order[-1])

    scatter_wait(dp, gh_mid, gh_in, gh_s, gh_r)
    gh_in[d] = gh_mid[d]
    few = tok // n_z
    each = sub // few
    for side in range(2):
        total = gh_in[0, side].astype(F32)
        for i in range(1, n_dp):
            total = total + gh_in[i, side].astype(F32)
        for i in range(each):
            zs_out[side * each + i] = total[i * few : (i + 1) * few, :].astype(BF16)
    scatter_start(alike, zs_out, zs_in, zs_s, zs_r)

    def head_step(block, carry):
        tokens = hid[block].reshape(tok, depth)
        head_acc[...] += jnp.dot(grads[block], tokens, preferred_element_type=F32)
        return carry

    head_acc[...] = jnp.zeros_like(head_acc)
    lax.fori_loop(0, n_dp, head_step, 0)
    head_out[...] = head_acc[...].astype(BF16)
    store_head = pltpu.make_async_copy(head_out, grad_head_hbm, local_sem.at[3])
    store_head.start()

    scatter_wait(alike, zs_out, zs_in, zs_s, zs_r)
    me = alike.me
    zs_in[me] = zs_out[me]
    total = zs_in[0].astype(F32)
    for i in range(1, alike.n):
        total = total + zs_in[i].astype(F32)
    fin[me] = total.astype(BF16)
    gather_start(alike, fin.at[me], fin, fa_s, fa_r)
    gather_wait(alike, fin.at[me], fin, fa_s, fa_r)

    def exchange(side):
        return ring.copy(
            fin.at[pl.ds(side * each, each)],
            fin_other.at[side],
            fo_s.at[side],
            fo_r.at[side],
            (up, down)[side],
        )

    for side in range(2):
        exchange(side).start()
    for side in range(2):
        for i in range(each):
            rows = slice(i * few, (i + 1) * few)
            grad_hidden_ref[2 * parity + side, rows, :] = fin[side * each + i].astype(F32)
    for side in range(2):
        exchange(side).wait()
        for i in range(each):
            rows = slice(i * few, (i + 1) * few)
            grad_hidden_ref[2 * (1 - parity) + side, rows, :] = fin_other[side, i].astype(F32)
    store_head.wait()


def copy_kernel(*refs):
    sources, results, held, (load, store) = refs[:3], refs[3:6], refs[6:9], refs[9:]
    loads = [pltpu.make_async_copy(a, b, load.at[i]) for i, (a, b) in enumerate(zip(sources, held))]
    stores = [pltpu.make_async_copy(a, b, store.at[i]) for i, (a, b) in enumerate(zip(held, results))]
    for copy in loads:
        copy.start()
    for before, after in zip(loads, stores):
        before.wait()
        after.start()
    for copy in stores:
        copy.wait()


def solution(mesh):
    n_dp, n_z, n_mp = mesh.shape["dp"], mesh.shape["vocab"], mesh.shape["mp"]
    n_zl = min(4, n_z)
    n_zh = n_z // n_zl

    def per_device(hidden, head_weight, teacher_logits, response_start):
        tok, depth = hidden.shape
        own, cols = teacher_logits.shape
        assert n_mp == 4 and own == 2 * tok == LEN and n_dp == 8 and n_zl == 4 and n_zh == 8
        few = tok // n_z
        dma = pltpu.SemaphoreType.DMA
        vmem = pl.BlockSpec(memory_space=pltpu.VMEM)
        hbm = pl.BlockSpec(memory_space=pl.ANY)
        shapes = (
            jax.ShapeDtypeStruct((1, own), F32),
            jax.ShapeDtypeStruct((4, tok // 4, depth), F32),
            jax.ShapeDtypeStruct((cols, depth), BF16),
        )
        results = pl.pallas_call(
            functools.partial(kernel, (n_dp, n_z, n_zl, n_zh)),
            name="distill",
            out_shape=shapes,
            in_specs=[hbm, hbm, hbm, pl.BlockSpec(memory_space=pltpu.SMEM)],
            out_specs=(vmem, vmem, hbm),
            scratch_shapes=[
                pltpu.VMEM((cols, depth), BF16),
                pltpu.VMEM((n_dp, cols, tok), BF16),
                pltpu.VMEM((cols, depth), BF16),
                pltpu.VMEM((n_dp, cols, tok), BF16),
                pltpu.VMEM((4, 2, 8, tok), F32),
                pltpu.VMEM((n_dp, 4, tok // 4, depth), BF16),
                pltpu.VMEM((4, 2, cols, tok), F32),
                pltpu.VMEM((4, cols, tok), F32),
                pltpu.VMEM((2, cols, tok), F32),
                pltpu.VMEM((2, cols, tok), F32),
                pltpu.VMEM((n_dp, 8, own), F32),
                pltpu.VMEM((n_zl, 8, own), F32),
                pltpu.VMEM((n_zh, 8, own), F32),
                pltpu.VMEM((n_dp, cols, tok), BF16),
                pltpu.VMEM((n_dp, 4, tok // 4, depth), BF16),
                pltpu.VMEM((n_dp, 2, tok // 4, depth), BF16),
                pltpu.VMEM((n_dp, 2, tok // 4, depth), BF16),
                pltpu.VMEM((n_dp, 2, tok // 4, depth), BF16),
                pltpu.VMEM((n_z // 2, few, depth), BF16),
                pltpu.VMEM((n_z // 2, few, depth), BF16),
                pltpu.VMEM((n_z // 2, few, depth), BF16),
                pltpu.VMEM((2, n_z // 4, few, depth), BF16),
                pltpu.VMEM((cols, depth), F32),
                dma((4,)),
                dma((2,)),
                pltpu.SemaphoreType.REGULAR((3,)),
                dma, dma,
                dma((2, n_dp // 2)), dma((n_dp,)),
                dma((n_dp, 2)), dma((n_dp, 2)),
                dma((4,)), dma((4,)),
                dma((2,)), dma((2,)),
                dma((n_dp,)), dma((n_dp,)),
                dma((n_zl,)), dma((n_zl,)),
                dma((n_zh,)), dma((n_zh,)),
                dma((3, 2)), dma((3, 2)),
                dma((3, 2)), dma((3, 2)),
                dma((4,)), dma((4,)),
                dma((n_dp, 2)), dma((n_dp, 2)),
                dma((n_dp,)), dma((n_dp,)),
                dma((n_z // 2,)), dma((n_z // 2,)),
                dma((n_z // 2,)), dma((n_z // 2,)),
                dma((2,)), dma((2,)),
            ],
            compiler_params=pltpu.CompilerParams(
                collective_id=0, has_side_effects=True, vmem_limit_bytes=56 << 20
            ),
        )(hidden.reshape(4, tok // 4, depth), head_weight.T, teacher_logits.T, response_start)
        kl, grad_hidden, grad_head = pl.pallas_call(
            copy_kernel,
            name="results",
            out_shape=shapes,
            in_specs=[hbm, hbm, hbm],
            out_specs=(hbm, hbm, hbm),
            scratch_shapes=[pltpu.VMEM(s.shape, s.dtype) for s in shapes] + [dma((3,)), dma((3,))],
        )(*results)
        return kl.reshape(own), grad_hidden.reshape(tok, depth), grad_head.T

    return jax.shard_map(
        per_device,
        mesh=mesh,
        in_specs=(P("dp", "mp"), P("mp", ("dp", "vocab")), P("mp", ("dp", "vocab")), P()),
        out_specs=(P("mp"), P("dp", "mp"), P("mp", ("dp", "vocab"))),
        check_vma=False,
    )
```

```python
import functools

import jax
import jax.numpy as jnp
from jax import lax
from jax.experimental import pallas as pl
from jax.experimental.pallas import tpu as pltpu
from jax.sharding import PartitionSpec as P

LEN = 256
MESH = pl.DeviceIdType.MESH
F32 = jnp.float32
BF16 = jnp.bfloat16

ROW_MS, ROW_SS, ROW_MT, ROW_ST, ROW_C = range(5)


class Group:
    def __init__(self, n, me, device):
        self.n, self.me, self.device = n, me, device

    def others(self):
        shifts = sorted(range(1, self.n), key=lambda k: -min(k, self.n - k))
        return [lax.rem(self.me + k, self.n) for k in shifts]

    def copy(self, src, dst, send, recv, to):
        return pltpu.make_async_remote_copy(
            src_ref=src,
            dst_ref=dst,
            send_sem=send,
            recv_sem=recv,
            device_id=self.device(to),
            device_id_type=MESH,
        )


def gather_start(group, src, held, send, recv):
    for peer in group.others():
        group.copy(src, held.at[group.me], send.at[peer], recv.at[group.me], peer).start()


def gather_wait(group, src, held, send, recv):
    for peer in group.others():
        copy = group.copy(src, held.at[peer], send.at[peer], recv.at[peer], peer)
        copy.wait_recv()
        copy.wait_send()


def scatter_start(group, parts, held, send, recv):
    for peer in group.others():
        group.copy(parts.at[peer], held.at[group.me], send.at[peer], recv.at[group.me], peer).start()


def scatter_wait(group, parts, held, send, recv):
    for peer in group.others():
        copy = group.copy(parts.at[peer], held.at[peer], send.at[peer], recv.at[peer], peer)
        copy.wait_recv()
        copy.wait_send()


def merge(held, n):
    rows = [[held[i, r : r + 1, :] for r in range(5)] for i in range(n)]
    top_s = functools.reduce(jnp.maximum, [row[ROW_MS] for row in rows])
    top_t = functools.reduce(jnp.maximum, [row[ROW_MT] for row in rows])
    sum_s = sum_t = cross = None
    for row in rows:
        scale_s = jnp.exp(row[ROW_MS] - top_s)
        scale_t = jnp.exp(row[ROW_MT] - top_t)
        terms = row[ROW_SS] * scale_s, row[ROW_ST] * scale_t, row[ROW_C] * scale_t
        if sum_s is None:
            sum_s, sum_t, cross = terms
        else:
            sum_s, sum_t, cross = sum_s + terms[0], sum_t + terms[1], cross + terms[2]
    return top_s, sum_s, top_t, sum_t, cross


def store_stats(ref, stats):
    for row, value in enumerate(stats):
        ref[row : row + 1, :] = value


def kernel(
    sizes,
    hidden_ref, head_hbm, teacher_hbm, start_ref,
    kl_ref, grad_hidden_ref, grad_head_hbm,
    head_ref, teacher_ref, head_out, student_exp, scales,
    hid, parts, swap_in, cross_out, cross_in,
    st_dp, st_zl, st_zh, grads, gh_out, gz_in, gh_mid, gh_in,
    zs_out, zs_in, fin, fin_other, head_acc,
    local_sem, teacher_sem, ready, hx_s, hx_r, hy_s, hy_r, hz_s, hz_r,
    swap_s, swap_r, cross_s, cross_r,
    sdp_s, sdp_r, szl_s, szl_r, szh_s, szh_r,
    t_s, t_r, e_s, e_r, sc_s, sc_r, gz_s, gz_r, gh_s, gh_r,
    zs_s, zs_r, fa_s, fa_r, fo_s, fo_r,
):
    n_dp, n_z, n_zl, n_zh = sizes
    n_y = n_dp // 2
    sub, depth = hidden_ref.shape[1:]
    tok = 4 * sub
    d, z, m = lax.axis_index("dp"), lax.axis_index("vocab"), lax.axis_index("mp")
    x, c = m // 2, m % 2
    y = d // 2
    partner = 2 * y + (1 - d % 2)
    zl, zh = z % n_zl, z // n_zl
    other_core, other_chip = 2 * x + (1 - c), 2 * (1 - x) + c
    diagonal = 2 * (1 - x) + (1 - c)
    parity = z % 2
    up, down = lax.rem(z + 1, n_z), lax.rem(z + n_z - 1, n_z)

    dp = Group(n_dp, d, lambda i: (i, z, m))
    column = Group(n_y, y, lambda i: (2 * i + d % 2, z, m))
    ring = Group(n_z, z, lambda i: (d, i, m))
    mine = 2 * (zl % 2) + zl // 2
    near = Group(n_zl, mine, lambda i: (d, zh * n_zl + 2 * (i % 2) + i // 2, m))
    alike = Group(n_z // 2, z // 2, lambda i: (d, 2 * i + parity, m))
    far = Group(n_zh, zh, lambda i: (d, i * n_zl + zl, m))
    mp = Group(4, m, lambda i: (d, z, i))
    far_next = [far.device(lax.rem(zh + k, n_zh)) for k in (1, n_zh - 1)]

    barrier = pltpu.get_barrier_semaphore()
    peers = [g.device(p) for g in (dp, near) for p in g.others()] + far_next
    peers += [mp.device(p) for p in mp.others()] + [ring.device(up), ring.device(down)]
    peers += [ring.device(lax.rem(z + k, n_z)) for k in (2, n_z - 2)]
    for peer in peers:
        pl.semaphore_signal(barrier, inc=1, device_id=peer, device_id_type=MESH)
    own = pltpu.make_async_copy(hidden_ref, hid.at[d], local_sem.at[0])
    own.start()
    load_head = pltpu.make_async_copy(head_hbm, head_ref, local_sem.at[1])
    load_head.start()
    load_teacher = [
        pltpu.make_async_copy(
            teacher_hbm.at[:, pl.ds(h * tok, tok)], teacher_ref.at[2 * m + h], teacher_sem.at[h]
        )
        for h in range(2)
    ]
    for load in load_teacher:
        load.start()
    own.wait()
    pl.semaphore_wait(barrier, len(peers))

    def tell(r):
        for peer in far_next:
            pl.semaphore_signal(ready.at[r], inc=1, device_id=peer, device_id_type=MESH)

    def hear(r):
        pl.semaphore_wait(ready.at[r], 2)

    half = pl.ds(2 * (z % 2), 2)

    def to_partner(block):
        part = hid.at[block, half]
        return dp.copy(part, part, hx_s, hx_r, partner)

    def to_column(block, peer):
        part = hid.at[block, half]
        return column.copy(part, part, hy_s.at[block % 2, peer], hy_r.at[block], peer)

    def to_ring(block, side, parity):
        part = hid.at[block, 2 * parity + side]
        return ring.copy(part, part, hz_s.at[block, side], hz_r.at[block, side], (up, down)[side])

    def pass_on(block):
        for side in range(2):
            to_ring(block, side, z % 2).start()

    class Spread:
        def __init__(self, held, send, recv):
            self.held, self.send, self.recv = held, send, recv

        def hop(self, way, block, h, to):
            part = self.held.at[block]
            return mp.copy(part, part, self.send.at[way, h], self.recv.at[way, h], to)

        def chip(self, h):
            return self.hop(0, 2 * m + h, h, other_chip)

        def core(self, h):
            return self.hop(1, 2 * m + h, h, other_core)

        def onward(self, h):
            return self.hop(2, 2 * other_chip + h, h, other_core)

        def start(self):
            for h in range(2):
                self.chip(h).start()
                self.core(h).start()

        def turn(self, h):
            self.chip(h).wait()
            self.onward(h).start()

        def finish(self):
            for h in range(2):
                self.core(h).wait()
                self.onward(h).wait()

    teacher = Spread(teacher_ref, t_s, t_r)
    student = Spread(student_exp, e_s, e_r)

    to_partner(d).start()
    for i in range(2):
        block = 2 * y + i

        @pl.when(block != d)
        def _():
            to_partner(partner).wait_recv()

        for peer in column.others():
            to_column(block, peer).start()
    pass_on(partner)
    tell(0)
    for load in load_teacher:
        load.wait()
    teacher.start()

    def blocks_of(i):
        return [2 * row + i for row in reversed(column.others())]

    def forward(i):
        for block in blocks_of(i):
            to_column(block, block // 2).wait_recv()
            pass_on(block)

    def arrive(i):
        for block in blocks_of(i):
            for side in range(2):
                to_ring(block, side, 1 - z % 2).wait_recv()

        @pl.when(2 * y + i != d)
        def _():
            for side in range(2):
                to_ring(partner, side, 1 - z % 2).wait_recv()

    def swap(k):
        return mp.copy(parts.at[k, 0], swap_in.at[k], swap_s.at[k], swap_r.at[k], other_core)

    def cross(k):
        return mp.copy(cross_out.at[k], cross_in.at[k], cross_s.at[k], cross_r.at[k], other_chip)

    def partial_sums(k):
        chip = jnp.where(k < 2, 1 - x, x)

        def one(j, carry):
            core = jnp.where(j == 0, 1 - c, c)
            block = hid[2 * (2 * chip + core) + k % 2].reshape(tok, depth)
            parts[k, j] = lax.dot_general(
                head_ref[...], block, (((1,), (1,)), ((), ())), preferred_element_type=F32
            )
            return carry

        lax.fori_loop(0, 2, one, 0)
        swap(k).start()

    def send_cross(k):
        swap(k).wait()
        cross_out[k] = parts[k, 1] + swap_in[k]
        cross(k).start()

    def student_step(k, carry):
        @pl.when(k == 0)
        def _():
            arrive(0)

        @pl.when(k == 1)
        def _():
            arrive(1)

        partial_sums(k)

        @pl.when(k == 0)
        def _():
            forward(1)

        @pl.when(k < 2)
        def _():
            send_cross(k)
            hear(k)
            tell(k + 1)

        return carry

    forward(0)
    load_head.wait()
    lax.fori_loop(0, 4, student_step, 0)
    for h in range(2):
        teacher.turn(h)

    for h in range(2):
        cols = slice(h * tok, (h + 1) * tok)
        swap(2 + h).wait()
        cross(h).wait()
        s = parts[2 + h, 1] + swap_in[2 + h] + cross_in[h]
        t = teacher_ref[2 * m + h].astype(F32)
        top_s = jnp.max(s, axis=0, keepdims=True)
        top_t = jnp.max(t, axis=0, keepdims=True)
        exp_s = jnp.exp(s - top_s)
        exp_t = jnp.exp(t - top_t)
        student_exp[2 * m + h] = exp_s.astype(BF16)
        stats = (
            top_s,
            jnp.sum(exp_s, axis=0, keepdims=True),
            top_t,
            jnp.sum(exp_t, axis=0, keepdims=True),
            jnp.sum(exp_t * (t - s), axis=0, keepdims=True),
        )
        for row, value in enumerate(stats):
            st_dp[d, row : row + 1, cols] = value

    to_partner(d).wait_send()
    for i in range(2):
        for peer in column.others():
            to_column(2 * y + i, peer).wait_send()
    for block in [partner] + blocks_of(0) + blocks_of(1):
        for side in range(2):
            to_ring(block, side, z % 2).wait_send()

    def share(group, held, send, recv, between=None):
        gather_start(group, held.at[group.me], held, send, recv)
        if between is not None:
            between()
        gather_wait(group, held.at[group.me], held, send, recv)
        return merge(held, group.n)

    def turns():
        for h in range(2):
            student.turn(h)
        teacher.finish()

    own_top_s = st_dp[d, ROW_MS : ROW_MS + 1, :]
    store_stats(st_zl.at[mine], share(dp, st_dp, sdp_s, sdp_r))
    student.start()
    store_stats(st_zh.at[zh], share(near, st_zl, szl_s, szl_r))
    hear(2)
    top_s, sum_s, top_t, sum_t, cross_term = share(far, st_zh, szh_s, szh_r, turns)
    position = lax.broadcasted_iota(jnp.int32, (1, 2 * tok), 1)
    mask = jnp.where(position >= start_ref[m], 1.0, 0.0).astype(F32)
    token_scales = mask * jnp.exp(own_top_s - top_s) / sum_s, mask / sum_t, top_t
    for h in range(2):
        for row, value in enumerate(token_scales):
            scales[m, h, row : row + 1, :] = value[:, h * tok : (h + 1) * tok]
    gather_start(mp, scales.at[m], scales, sc_s, sc_r)
    kl_ref[...] = mask * (cross_term / sum_t - top_t - jnp.log(sum_t) + top_s + jnp.log(sum_s))

    def logit_grads(block):
        scale_s, scale_t, top = [scales[block // 2, block % 2, row : row + 1, :] for row in range(3)]
        exp_t = jnp.exp(teacher_ref[block].astype(F32) - top)
        grads[block] = (student_exp[block].astype(F32) * scale_s - exp_t * scale_t).astype(BF16)

    def to_neighbour(block, side):
        return ring.copy(
            gh_out.at[block, 2 * (1 - parity) + side],
            gz_in.at[block, side],
            gz_s.at[block, side],
            gz_r.at[block, side],
            (up, down)[side],
        )

    def owner_copy(block):
        return dp.copy(gh_mid.at[block], gh_in.at[d], gh_s.at[block], gh_r.at[d], block)

    def hidden_terms(block):
        logit_grads(block)
        gh_out[block] = (
            lax.dot_general(
                grads[block], head_ref[...], (((0,), (0,)), ((), ())), preferred_element_type=F32
            )
            .astype(BF16)
            .reshape(4, sub, depth)
        )
        for side in range(2):
            to_neighbour(block, side).start()

    def hand_over(block):
        for side in range(2):
            to_neighbour(block, side).wait()
            own_rows = gh_out[block, 2 * parity + side].astype(F32)
            gh_mid[block, side] = (own_rows + gz_in[block, side].astype(F32)).astype(BF16)

        @pl.when(block != d)
        def _():
            owner_copy(block).start()

    student.finish()
    gather_wait(mp, scales.at[m], scales, sc_s, sc_r)
    def block_at(i):
        pair = i // 2
        rows_away = jnp.where(pair == 3, 0, jnp.where(pair == 2, 3, 2 - pair))
        return 2 * ((y + rows_away) % n_y) + (d + 1 + i) % 2

    def grad_step(i, carry):
        hidden_terms(block_at(i))

        @pl.when(i > 0)
        def _():
            hand_over(block_at(i - 1))

        return carry

    lax.fori_loop(0, n_dp, grad_step, 0)
    hand_over(block_at(n_dp - 1))

    scatter_wait(dp, gh_mid, gh_in, gh_s, gh_r)
    gh_in[d] = gh_mid[d]
    few = tok // n_z
    each = sub // few
    for side in range(2):
        total = gh_in[0, side].astype(F32)
        for i in range(1, n_dp):
            total = total + gh_in[i, side].astype(F32)
        for i in range(each):
            zs_out[side * each + i] = total[i * few : (i + 1) * few, :].astype(BF16)
    scatter_start(alike, zs_out, zs_in, zs_s, zs_r)

    def head_step(block, carry):
        tokens = hid[block].reshape(tok, depth)
        head_acc[...] += jnp.dot(grads[block], tokens, preferred_element_type=F32)
        return carry

    head_acc[...] = jnp.zeros_like(head_acc)
    lax.fori_loop(0, n_dp, head_step, 0)
    head_out[...] = head_acc[...].astype(BF16)
    store_head = pltpu.make_async_copy(head_out, grad_head_hbm, local_sem.at[3])
    store_head.start()

    scatter_wait(alike, zs_out, zs_in, zs_s, zs_r)
    me = alike.me
    zs_in[me] = zs_out[me]
    total = zs_in[0].astype(F32)
    for i in range(1, alike.n):
        total = total + zs_in[i].astype(F32)
    fin[me] = total.astype(BF16)
    gather_start(alike, fin.at[me], fin, fa_s, fa_r)
    gather_wait(alike, fin.at[me], fin, fa_s, fa_r)

    def exchange(side):
        return ring.copy(
            fin.at[pl.ds(side * each, each)],
            fin_other.at[side],
            fo_s.at[side],
            fo_r.at[side],
            (up, down)[side],
        )

    for side in range(2):
        exchange(side).start()
    for side in range(2):
        for i in range(each):
            rows = slice(i * few, (i + 1) * few)
            grad_hidden_ref[2 * parity + side, rows, :] = fin[side * each + i].astype(F32)
    for side in range(2):
        exchange(side).wait()
        for i in range(each):
            rows = slice(i * few, (i + 1) * few)
            grad_hidden_ref[2 * (1 - parity) + side, rows, :] = fin_other[side, i].astype(F32)
    store_head.wait()


def copy_kernel(*refs):
    sources, results, held, (load, store) = refs[:3], refs[3:6], refs[6:9], refs[9:]
    loads = [pltpu.make_async_copy(a, b, load.at[i]) for i, (a, b) in enumerate(zip(sources, held))]
    stores = [pltpu.make_async_copy(a, b, store.at[i]) for i, (a, b) in enumerate(zip(held, results))]
    for copy in loads:
        copy.start()
    for before, after in zip(loads, stores):
        before.wait()
        after.start()
    for copy in stores:
        copy.wait()


def solution(mesh):
    n_dp, n_z, n_mp = mesh.shape["dp"], mesh.shape["vocab"], mesh.shape["mp"]
    n_zl = min(4, n_z)
    n_zh = n_z // n_zl

    def per_device(hidden, head_weight, teacher_logits, response_start):
        tok, depth = hidden.shape
        own, cols = teacher_logits.shape
        assert n_mp == 4 and own == 2 * tok == LEN and n_dp == 8 and n_zl == 4 and n_zh == 8
        few = tok // n_z
        dma = pltpu.SemaphoreType.DMA
        vmem = pl.BlockSpec(memory_space=pltpu.VMEM)
        hbm = pl.BlockSpec(memory_space=pl.ANY)
        shapes = (
            jax.ShapeDtypeStruct((1, own), F32),
            jax.ShapeDtypeStruct((4, tok // 4, depth), F32),
            jax.ShapeDtypeStruct((cols, depth), BF16),
        )
        results = pl.pallas_call(
            functools.partial(kernel, (n_dp, n_z, n_zl, n_zh)),
            name="distill",
            out_shape=shapes,
            in_specs=[hbm, hbm, hbm, pl.BlockSpec(memory_space=pltpu.SMEM)],
            out_specs=(vmem, vmem, hbm),
            scratch_shapes=[
                pltpu.VMEM((cols, depth), BF16),
                pltpu.VMEM((n_dp, cols, tok), BF16),
                pltpu.VMEM((cols, depth), BF16),
                pltpu.VMEM((n_dp, cols, tok), BF16),
                pltpu.VMEM((4, 2, 8, tok), F32),
                pltpu.VMEM((n_dp, 4, tok // 4, depth), BF16),
                pltpu.VMEM((4, 2, cols, tok), F32),
                pltpu.VMEM((4, cols, tok), F32),
                pltpu.VMEM((2, cols, tok), F32),
                pltpu.VMEM((2, cols, tok), F32),
                pltpu.VMEM((n_dp, 8, own), F32),
                pltpu.VMEM((n_zl, 8, own), F32),
                pltpu.VMEM((n_zh, 8, own), F32),
                pltpu.VMEM((n_dp, cols, tok), BF16),
                pltpu.VMEM((n_dp, 4, tok // 4, depth), BF16),
                pltpu.VMEM((n_dp, 2, tok // 4, depth), BF16),
                pltpu.VMEM((n_dp, 2, tok // 4, depth), BF16),
                pltpu.VMEM((n_dp, 2, tok // 4, depth), BF16),
                pltpu.VMEM((n_z // 2, few, depth), BF16),
                pltpu.VMEM((n_z // 2, few, depth), BF16),
                pltpu.VMEM((n_z // 2, few, depth), BF16),
                pltpu.VMEM((2, n_z // 4, few, depth), BF16),
                pltpu.VMEM((cols, depth), F32),
                dma((4,)),
                dma((2,)),
                pltpu.SemaphoreType.REGULAR((3,)),
                dma, dma,
                dma((2, n_dp // 2)), dma((n_dp,)),
                dma((n_dp, 2)), dma((n_dp, 2)),
                dma((4,)), dma((4,)),
                dma((2,)), dma((2,)),
                dma((n_dp,)), dma((n_dp,)),
                dma((n_zl,)), dma((n_zl,)),
                dma((n_zh,)), dma((n_zh,)),
                dma((3, 2)), dma((3, 2)),
                dma((3, 2)), dma((3, 2)),
                dma((4,)), dma((4,)),
                dma((n_dp, 2)), dma((n_dp, 2)),
                dma((n_dp,)), dma((n_dp,)),
                dma((n_z // 2,)), dma((n_z // 2,)),
                dma((n_z // 2,)), dma((n_z // 2,)),
                dma((2,)), dma((2,)),
            ],
            compiler_params=pltpu.CompilerParams(
                collective_id=0, has_side_effects=True, vmem_limit_bytes=56 << 20
            ),
        )(hidden.reshape(4, tok // 4, depth), head_weight.T, teacher_logits.T, response_start)
        kl, grad_hidden, grad_head = pl.pallas_call(
            copy_kernel,
            name="results",
            out_shape=shapes,
            in_specs=[hbm, hbm, hbm],
            out_specs=(hbm, hbm, hbm),
            scratch_shapes=[pltpu.VMEM(s.shape, s.dtype) for s in shapes] + [dma((3,)), dma((3,))],
        )(*results)
        return kl.reshape(own), grad_hidden.reshape(tok, depth), grad_head.T

    return jax.shard_map(
        per_device,
        mesh=mesh,
        in_specs=(P("dp", "mp"), P("mp", ("dp", "vocab")), P("mp", ("dp", "vocab")), P()),
        out_specs=(P("mp"), P("dp", "mp"), P("mp", ("dp", "vocab"))),
        check_vma=False,
    )
```

```python
import functools

import jax
import jax.numpy as jnp
from jax import lax
from jax.experimental import pallas as pl
from jax.experimental.pallas import tpu as pltpu
from jax.sharding import PartitionSpec as P

LEN = 256
MESH = pl.DeviceIdType.MESH
F32 = jnp.float32
BF16 = jnp.bfloat16

ROW_MS, ROW_SS, ROW_MT, ROW_ST, ROW_C = range(5)


class Group:
    def __init__(self, n, me, device):
        self.n, self.me, self.device = n, me, device

    def others(self):
        shifts = sorted(range(1, self.n), key=lambda k: -min(k, self.n - k))
        return [lax.rem(self.me + k, self.n) for k in shifts]

    def copy(self, src, dst, send, recv, to):
        return pltpu.make_async_remote_copy(
            src_ref=src,
            dst_ref=dst,
            send_sem=send,
            recv_sem=recv,
            device_id=self.device(to),
            device_id_type=MESH,
        )


def gather_start(group, src, held, send, recv):
    for peer in group.others():
        group.copy(src, held.at[group.me], send.at[peer], recv.at[group.me], peer).start()


def gather_wait(group, src, held, send, recv):
    for peer in group.others():
        copy = group.copy(src, held.at[peer], send.at[peer], recv.at[peer], peer)
        copy.wait_recv()
        copy.wait_send()


def scatter_start(group, parts, held, send, recv):
    for peer in group.others():
        group.copy(parts.at[peer], held.at[group.me], send.at[peer], recv.at[group.me], peer).start()


def scatter_wait(group, parts, held, send, recv):
    for peer in group.others():
        copy = group.copy(parts.at[peer], held.at[peer], send.at[peer], recv.at[peer], peer)
        copy.wait_recv()
        copy.wait_send()


def merge(held, n):
    rows = [[held[i, r : r + 1, :] for r in range(5)] for i in range(n)]
    top_s = functools.reduce(jnp.maximum, [row[ROW_MS] for row in rows])
    top_t = functools.reduce(jnp.maximum, [row[ROW_MT] for row in rows])
    sum_s = sum_t = cross = None
    for row in rows:
        scale_s = jnp.exp(row[ROW_MS] - top_s)
        scale_t = jnp.exp(row[ROW_MT] - top_t)
        terms = row[ROW_SS] * scale_s, row[ROW_ST] * scale_t, row[ROW_C] * scale_t
        if sum_s is None:
            sum_s, sum_t, cross = terms
        else:
            sum_s, sum_t, cross = sum_s + terms[0], sum_t + terms[1], cross + terms[2]
    return top_s, sum_s, top_t, sum_t, cross


def store_stats(ref, stats):
    for row, value in enumerate(stats):
        ref[row : row + 1, :] = value


def kernel(
    sizes,
    hidden_ref, head_hbm, teacher_hbm, start_ref,
    kl_ref, grad_hidden_ref, grad_head_hbm,
    head_ref, teacher_ref, head_out, student_exp, scales,
    hid, parts, swap_in, cross_out, cross_in,
    st_dp, st_zl, st_zh, grads, gh_out, gz_in, gh_mid, gh_in,
    zs_out, zs_in, fin, fin_other, head_acc,
    local_sem, teacher_sem, ready, hx_s, hx_r, hy_s, hy_r, hz_s, hz_r,
    swap_s, swap_r, cross_s, cross_r,
    sdp_s, sdp_r, szl_s, szl_r, szh_s, szh_r,
    t_s, t_r, e_s, e_r, sc_s, sc_r, gz_s, gz_r, gh_s, gh_r,
    zs_s, zs_r, fa_s, fa_r, fo_s, fo_r,
):
    n_dp, n_z, n_zl, n_zh = sizes
    n_y = n_dp // 2
    sub, depth = hidden_ref.shape[1:]
    tok = 4 * sub
    d, z, m = lax.axis_index("dp"), lax.axis_index("vocab"), lax.axis_index("mp")
    x, c = m // 2, m % 2
    y = d // 2
    partner = 2 * y + (1 - d % 2)
    zl, zh = z % n_zl, z // n_zl
    other_core, other_chip = 2 * x + (1 - c), 2 * (1 - x) + c
    diagonal = 2 * (1 - x) + (1 - c)
    parity = z % 2
    up, down = lax.rem(z + 1, n_z), lax.rem(z + n_z - 1, n_z)

    dp = Group(n_dp, d, lambda i: (i, z, m))
    column = Group(n_y, y, lambda i: (2 * i + d % 2, z, m))
    ring = Group(n_z, z, lambda i: (d, i, m))
    mine = 2 * (zl % 2) + zl // 2
    near = Group(n_zl, mine, lambda i: (d, zh * n_zl + 2 * (i % 2) + i // 2, m))
    alike = Group(n_z // 2, z // 2, lambda i: (d, 2 * i + parity, m))
    far = Group(n_zh, zh, lambda i: (d, i * n_zl + zl, m))
    mp = Group(4, m, lambda i: (d, z, i))
    far_next = [far.device(lax.rem(zh + k, n_zh)) for k in (1, n_zh - 1)]

    barrier = pltpu.get_barrier_semaphore()
    peers = [g.device(p) for g in (dp, near) for p in g.others()] + far_next
    peers += [mp.device(p) for p in mp.others()] + [ring.device(up), ring.device(down)]
    peers += [ring.device(lax.rem(z + k, n_z)) for k in (2, n_z - 2)]
    for peer in peers:
        pl.semaphore_signal(barrier, inc=1, device_id=peer, device_id_type=MESH)
    own = pltpu.make_async_copy(hidden_ref, hid.at[d], local_sem.at[0])
    own.start()
    load_head = pltpu.make_async_copy(head_hbm, head_ref, local_sem.at[1])
    load_head.start()
    load_teacher = [
        pltpu.make_async_copy(
            teacher_hbm.at[:, pl.ds(h * tok, tok)], teacher_ref.at[2 * m + h], teacher_sem.at[h]
        )
        for h in range(2)
    ]
    for load in load_teacher:
        load.start()
    own.wait()
    pl.semaphore_wait(barrier, len(peers))

    def tell(r):
        for peer in far_next:
            pl.semaphore_signal(ready.at[r], inc=1, device_id=peer, device_id_type=MESH)

    def hear(r):
        pl.semaphore_wait(ready.at[r], 2)

    half = pl.ds(2 * (z % 2), 2)

    def to_partner(block):
        part = hid.at[block, half]
        return dp.copy(part, part, hx_s, hx_r, partner)

    def to_column(block, peer):
        part = hid.at[block, half]
        return column.copy(part, part, hy_s.at[block % 2, peer], hy_r.at[block], peer)

    def to_ring(block, side, parity):
        part = hid.at[block, 2 * parity + side]
        return ring.copy(part, part, hz_s.at[block, side], hz_r.at[block, side], (up, down)[side])

    def pass_on(block):
        for side in range(2):
            to_ring(block, side, z % 2).start()

    class Spread:
        def __init__(self, held, send, recv):
            self.held, self.send, self.recv = held, send, recv

        def hop(self, way, block, h, to):
            part = self.held.at[block]
            return mp.copy(part, part, self.send.at[way, h], self.recv.at[way, h], to)

        def chip(self, h):
            return self.hop(0, 2 * m + h, h, other_chip)

        def core(self, h):
            return self.hop(1, 2 * m + h, h, other_core)

        def onward(self, h):
            return self.hop(2, 2 * other_chip + h, h, other_core)

        def start(self):
            for h in range(2):
                self.chip(h).start()
                self.core(h).start()

        def turn(self, h):
            self.chip(h).wait()
            self.onward(h).start()

        def finish(self):
            for h in range(2):
                self.core(h).wait()
                self.onward(h).wait()

    teacher = Spread(teacher_ref, t_s, t_r)
    student = Spread(student_exp, e_s, e_r)

    to_partner(d).start()
    for i in range(2):
        block = 2 * y + i

        @pl.when(block != d)
        def _():
            to_partner(partner).wait_recv()

        for peer in column.others():
            to_column(block, peer).start()
    pass_on(partner)
    tell(0)
    for load in load_teacher:
        load.wait()
    teacher.start()

    def blocks_of(i):
        return [2 * row + i for row in reversed(column.others())]

    def forward(i):
        for block in blocks_of(i):
            to_column(block, block // 2).wait_recv()
            pass_on(block)

    def arrive(i):
        for block in blocks_of(i):
            for side in range(2):
                to_ring(block, side, 1 - z % 2).wait_recv()

        @pl.when(2 * y + i != d)
        def _():
            for side in range(2):
                to_ring(partner, side, 1 - z % 2).wait_recv()

    def swap(k):
        return mp.copy(parts.at[k, 0], swap_in.at[k], swap_s.at[k], swap_r.at[k], other_core)

    def cross(k):
        return mp.copy(cross_out.at[k], cross_in.at[k], cross_s.at[k], cross_r.at[k], other_chip)

    def partial_sums(k):
        chip = jnp.where(k < 2, 1 - x, x)

        def one(j, carry):
            core = jnp.where(j == 0, 1 - c, c)
            block = hid[2 * (2 * chip + core) + k % 2].reshape(tok, depth)
            parts[k, j] = lax.dot_general(
                head_ref[...], block, (((1,), (1,)), ((), ())), preferred_element_type=F32
            )
            return carry

        lax.fori_loop(0, 2, one, 0)
        swap(k).start()

    def send_cross(k):
        swap(k).wait()
        cross_out[k] = parts[k, 1] + swap_in[k]
        cross(k).start()

    def student_step(k, carry):
        @pl.when(k == 0)
        def _():
            arrive(0)

        @pl.when(k == 1)
        def _():
            arrive(1)

        partial_sums(k)

        @pl.when(k == 0)
        def _():
            forward(1)

        @pl.when(k < 2)
        def _():
            send_cross(k)
            hear(k)
            tell(k + 1)

        return carry

    forward(0)
    load_head.wait()
    lax.fori_loop(0, 4, student_step, 0)
    for h in range(2):
        teacher.turn(h)

    for h in range(2):
        cols = slice(h * tok, (h + 1) * tok)
        swap(2 + h).wait()
        cross(h).wait()
        s = parts[2 + h, 1] + swap_in[2 + h] + cross_in[h]
        t = teacher_ref[2 * m + h].astype(F32)
        top_s = jnp.max(s, axis=0, keepdims=True)
        top_t = jnp.max(t, axis=0, keepdims=True)
        exp_s = jnp.exp(s - top_s)
        exp_t = jnp.exp(t - top_t)
        student_exp[2 * m + h] = exp_s.astype(BF16)
        stats = (
            top_s,
            jnp.sum(exp_s, axis=0, keepdims=True),
            top_t,
            jnp.sum(exp_t, axis=0, keepdims=True),
            jnp.sum(exp_t * (t - s), axis=0, keepdims=True),
        )
        for row, value in enumerate(stats):
            st_dp[d, row : row + 1, cols] = value

    to_partner(d).wait_send()
    for i in range(2):
        for peer in column.others():
            to_column(2 * y + i, peer).wait_send()
    for block in [partner] + blocks_of(0) + blocks_of(1):
        for side in range(2):
            to_ring(block, side, z % 2).wait_send()

    def share(group, held, send, recv, between=None):
        gather_start(group, held.at[group.me], held, send, recv)
        if between is not None:
            between()
        gather_wait(group, held.at[group.me], held, send, recv)
        return merge(held, group.n)

    def turns():
        for h in range(2):
            student.turn(h)
        teacher.finish()

    own_top_s = st_dp[d, ROW_MS : ROW_MS + 1, :]
    store_stats(st_zl.at[mine], share(dp, st_dp, sdp_s, sdp_r))
    student.start()
    store_stats(st_zh.at[zh], share(near, st_zl, szl_s, szl_r))
    hear(2)
    top_s, sum_s, top_t, sum_t, cross_term = share(far, st_zh, szh_s, szh_r, turns)
    position = lax.broadcasted_iota(jnp.int32, (1, 2 * tok), 1)
    mask = jnp.where(position >= start_ref[m], 1.0, 0.0).astype(F32)
    token_scales = mask * jnp.exp(own_top_s - top_s) / sum_s, mask / sum_t, top_t
    for h in range(2):
        for row, value in enumerate(token_scales):
            scales[m, h, row : row + 1, :] = value[:, h * tok : (h + 1) * tok]
    gather_start(mp, scales.at[m], scales, sc_s, sc_r)
    kl_ref[...] = mask * (cross_term / sum_t - top_t - jnp.log(sum_t) + top_s + jnp.log(sum_s))

    def logit_grads(block):
        scale_s, scale_t, top = [scales[block // 2, block % 2, row : row + 1, :] for row in range(3)]
        exp_t = jnp.exp(teacher_ref[block].astype(F32) - top)
        grads[block] = (student_exp[block].astype(F32) * scale_s - exp_t * scale_t).astype(BF16)

    def to_neighbour(block, side):
        return ring.copy(
            gh_out.at[block, 2 * (1 - parity) + side],
            gz_in.at[block, side],
            gz_s.at[block, side],
            gz_r.at[block, side],
            (up, down)[side],
        )

    def owner_copy(block):
        return dp.copy(gh_mid.at[block], gh_in.at[d], gh_s.at[block], gh_r.at[d], block)

    def hidden_terms(block):
        logit_grads(block)
        gh_out[block] = (
            lax.dot_general(
                grads[block], head_ref[...], (((0,), (0,)), ((), ())), preferred_element_type=F32
            )
            .astype(BF16)
            .reshape(4, sub, depth)
        )
        for side in range(2):
            to_neighbour(block, side).start()

    def hand_over(block):
        for side in range(2):
            to_neighbour(block, side).wait()
            own_rows = gh_out[block, 2 * parity + side].astype(F32)
            gh_mid[block, side] = (own_rows + gz_in[block, side].astype(F32)).astype(BF16)

        @pl.when(block != d)
        def _():
            owner_copy(block).start()

    student.finish()
    gather_wait(mp, scales.at[m], scales, sc_s, sc_r)
    def block_at(i):
        pair = i // 2
        rows_away = jnp.where(pair == 3, 0, jnp.where(pair == 2, 3, 2 - pair))
        return 2 * ((y + rows_away) % n_y) + (d + 1 + i) % 2

    def grad_step(i, carry):
        hidden_terms(block_at(i))

        @pl.when(i > 0)
        def _():
            hand_over(block_at(i - 1))

        return carry

    lax.fori_loop(0, n_dp, grad_step, 0)
    hand_over(block_at(n_dp - 1))

    scatter_wait(dp, gh_mid, gh_in, gh_s, gh_r)
    gh_in[d] = gh_mid[d]
    few = tok // n_z
    each = sub // few
    for side in range(2):
        total = gh_in[0, side].astype(F32)
        for i in range(1, n_dp):
            total = total + gh_in[i, side].astype(F32)
        for i in range(each):
            zs_out[side * each + i] = total[i * few : (i + 1) * few, :].astype(BF16)
    scatter_start(alike, zs_out, zs_in, zs_s, zs_r)

    def head_step(block, carry):
        tokens = hid[block].reshape(tok, depth)
        head_acc[...] += jnp.dot(grads[block], tokens, preferred_element_type=F32)
        return carry

    head_acc[...] = jnp.dot(grads[0], hid[0].reshape(tok, depth), preferred_element_type=F32)
    lax.fori_loop(1, n_dp, head_step, 0)
    head_out[...] = head_acc[...].astype(BF16)
    store_head = pltpu.make_async_copy(head_out, grad_head_hbm, local_sem.at[3])
    store_head.start()

    scatter_wait(alike, zs_out, zs_in, zs_s, zs_r)
    me = alike.me
    zs_in[me] = zs_out[me]
    total = zs_in[0].astype(F32)
    for i in range(1, alike.n):
        total = total + zs_in[i].astype(F32)
    fin[me] = total.astype(BF16)
    gather_start(alike, fin.at[me], fin, fa_s, fa_r)
    gather_wait(alike, fin.at[me], fin, fa_s, fa_r)

    def exchange(side):
        return ring.copy(
            fin.at[pl.ds(side * each, each)],
            fin_other.at[side],
            fo_s.at[side],
            fo_r.at[side],
            (up, down)[side],
        )

    for side in range(2):
        exchange(side).start()
    for side in range(2):
        for i in range(each):
            rows = slice(i * few, (i + 1) * few)
            grad_hidden_ref[2 * parity + side, rows, :] = fin[side * each + i].astype(F32)
    for side in range(2):
        exchange(side).wait()
        for i in range(each):
            rows = slice(i * few, (i + 1) * few)
            grad_hidden_ref[2 * (1 - parity) + side, rows, :] = fin_other[side, i].astype(F32)
    store_head.wait()


def copy_kernel(*refs):
    sources, results, held, (load, store) = refs[:3], refs[3:6], refs[6:9], refs[9:]
    loads = [pltpu.make_async_copy(a, b, load.at[i]) for i, (a, b) in enumerate(zip(sources, held))]
    stores = [pltpu.make_async_copy(a, b, store.at[i]) for i, (a, b) in enumerate(zip(held, results))]
    for copy in loads:
        copy.start()
    for before, after in zip(loads, stores):
        before.wait()
        after.start()
    for copy in stores:
        copy.wait()


def solution(mesh):
    n_dp, n_z, n_mp = mesh.shape["dp"], mesh.shape["vocab"], mesh.shape["mp"]
    n_zl = min(4, n_z)
    n_zh = n_z // n_zl

    def per_device(hidden, head_weight, teacher_logits, response_start):
        tok, depth = hidden.shape
        own, cols = teacher_logits.shape
        assert n_mp == 4 and own == 2 * tok == LEN and n_dp == 8 and n_zl == 4 and n_zh == 8
        few = tok // n_z
        dma = pltpu.SemaphoreType.DMA
        vmem = pl.BlockSpec(memory_space=pltpu.VMEM)
        hbm = pl.BlockSpec(memory_space=pl.ANY)
        shapes = (
            jax.ShapeDtypeStruct((1, own), F32),
            jax.ShapeDtypeStruct((4, tok // 4, depth), F32),
            jax.ShapeDtypeStruct((cols, depth), BF16),
        )
        results = pl.pallas_call(
            functools.partial(kernel, (n_dp, n_z, n_zl, n_zh)),
            name="distill",
            out_shape=shapes,
            in_specs=[hbm, hbm, hbm, pl.BlockSpec(memory_space=pltpu.SMEM)],
            out_specs=(vmem, vmem, hbm),
            scratch_shapes=[
                pltpu.VMEM((cols, depth), BF16),
                pltpu.VMEM((n_dp, cols, tok), BF16),
                pltpu.VMEM((cols, depth), BF16),
                pltpu.VMEM((n_dp, cols, tok), BF16),
                pltpu.VMEM((4, 2, 8, tok), F32),
                pltpu.VMEM((n_dp, 4, tok // 4, depth), BF16),
                pltpu.VMEM((4, 2, cols, tok), F32),
                pltpu.VMEM((4, cols, tok), F32),
                pltpu.VMEM((2, cols, tok), F32),
                pltpu.VMEM((2, cols, tok), F32),
                pltpu.VMEM((n_dp, 8, own), F32),
                pltpu.VMEM((n_zl, 8, own), F32),
                pltpu.VMEM((n_zh, 8, own), F32),
                pltpu.VMEM((n_dp, cols, tok), BF16),
                pltpu.VMEM((n_dp, 4, tok // 4, depth), BF16),
                pltpu.VMEM((n_dp, 2, tok // 4, depth), BF16),
                pltpu.VMEM((n_dp, 2, tok // 4, depth), BF16),
                pltpu.VMEM((n_dp, 2, tok // 4, depth), BF16),
                pltpu.VMEM((n_z // 2, few, depth), BF16),
                pltpu.VMEM((n_z // 2, few, depth), BF16),
                pltpu.VMEM((n_z // 2, few, depth), BF16),
                pltpu.VMEM((2, n_z // 4, few, depth), BF16),
                pltpu.VMEM((cols, depth), F32),
                dma((4,)),
                dma((2,)),
                pltpu.SemaphoreType.REGULAR((3,)),
                dma, dma,
                dma((2, n_dp // 2)), dma((n_dp,)),
                dma((n_dp, 2)), dma((n_dp, 2)),
                dma((4,)), dma((4,)),
                dma((2,)), dma((2,)),
                dma((n_dp,)), dma((n_dp,)),
                dma((n_zl,)), dma((n_zl,)),
                dma((n_zh,)), dma((n_zh,)),
                dma((3, 2)), dma((3, 2)),
                dma((3, 2)), dma((3, 2)),
                dma((4,)), dma((4,)),
                dma((n_dp, 2)), dma((n_dp, 2)),
                dma((n_dp,)), dma((n_dp,)),
                dma((n_z // 2,)), dma((n_z // 2,)),
                dma((n_z // 2,)), dma((n_z // 2,)),
                dma((2,)), dma((2,)),
            ],
            compiler_params=pltpu.CompilerParams(
                collective_id=0, has_side_effects=True, vmem_limit_bytes=56 << 20
            ),
        )(hidden.reshape(4, tok // 4, depth), head_weight.T, teacher_logits.T, response_start)
        kl, grad_hidden, grad_head = pl.pallas_call(
            copy_kernel,
            name="results",
            out_shape=shapes,
            in_specs=[hbm, hbm, hbm],
            out_specs=(hbm, hbm, hbm),
            scratch_shapes=[pltpu.VMEM(s.shape, s.dtype) for s in shapes] + [dma((3,)), dma((3,))],
        )(*results)
        return kl.reshape(own), grad_hidden.reshape(tok, depth), grad_head.T

    return jax.shard_map(
        per_device,
        mesh=mesh,
        in_specs=(P("dp", "mp"), P("mp", ("dp", "vocab")), P("mp", ("dp", "vocab")), P()),
        out_specs=(P("mp"), P("dp", "mp"), P("mp", ("dp", "vocab"))),
        check_vma=False,
    )
```
